32 devices in a mesh: heads: 4 (over y, x), seq: 8 (over z, core).
Axes of the slice: x: 2, y: 2, z: 4, core: 2. Of those that a mesh axis runs over, the one named last changes fastest.
Arguments:
- local_qkv: bfloat16 [3, 4096, 2048], P(None, 'seq', 'heads'), may hold values from -8 to 8
- routed_qkv: bfloat16 [3, 4096, 2048], P(None, 'seq', 'heads'), may hold values from -8 to 8
- clusters: int32 [16, 4096], P('heads', 'seq'), may hold values from 0 to 127, as said below
- wo_local: bfloat16 [2048, 4096], P('heads'), may hold values from -0.5 to 0.5
- wo_routed: bfloat16 [2048, 4096], P('heads'), may hold values from -0.5 to 0.5
Outputs:
- layer_out: bfloat16 [4096, 4096], P('seq', 'heads')
The draws below stay inside these ranges and needn't reach their ends.
Inputs may be any that keep to these rules, and one draw needn't show every extreme that they name: `clusters`: in every routed head, no cluster holds more than 8 of the 512 tokens of one aligned block of tokens; in every head and block some cluster holds exactly 8 of them.
All inputs are finite; a program needn't handle non-finite values.
Results may differ from the reference program's by a relative error of at most 0.009.
Values may be sent and summed in bfloat16 or wider, within the bound.
A program may use at most 128 MiB of HBM per device.

```python
import jax
import jax.numpy as jnp
from jax import lax

D = 4096
DH = 128
LOCAL_HEADS = 16
ROUTED_HEADS = 16
TOK_DEV = 512
WINDOW = 512
NCLUST = 128
MOST = 8
TOKENS = 4096
N_HEADS = 4
N_SEQ = 8


def cluster_table(base_key):
    block_count = TOKENS // TOK_DEV
    slot_count = NCLUST * MOST
    order_key, noise_key, shuffle_key = jax.random.split(base_key, 3)
    priority = jax.vmap(lambda k: jax.random.permutation(k, NCLUST))(jax.random.split(order_key, ROUTED_HEADS)).astype(jnp.int32)
    labels = jnp.arange(slot_count, dtype=jnp.int32) // MOST
    ranked = priority[:, labels]
    noise = jax.random.randint(noise_key, (ROUTED_HEADS, block_count, slot_count), 0, NCLUST)
    scored = ranked[:, None, :] * 2 + noise
    scored = jnp.where(ranked[:, None, :] == 0, -1, scored)
    scored = scored * 16384 + jnp.arange(slot_count, dtype=jnp.int32)
    picked = jnp.argsort(scored, axis=-1)[..., :TOK_DEV]
    chosen = labels[picked]
    shuffles = jax.vmap(lambda k: jax.random.permutation(k, TOK_DEV))(jax.random.split(shuffle_key, ROUTED_HEADS * block_count))
    shuffles = shuffles.reshape(ROUTED_HEADS, block_count, TOK_DEV)
    chosen = jnp.take_along_axis(chosen, shuffles, axis=-1)
    return chosen.reshape(ROUTED_HEADS, TOKENS).astype(jnp.int32)


def float_base(base_key, shape):
    return jnp.clip(jax.random.normal(base_key, shape, jnp.float32), -4.5, 4.5)


def draw_local_qkv(key, part):
    width = LOCAL_HEADS * DH
    base = float_base(jax.random.fold_in(key, 1), (3, TOKENS, width))
    return base.astype(jnp.bfloat16)


def draw_routed_qkv(key, part):
    width = ROUTED_HEADS * DH
    base = float_base(jax.random.fold_in(key, 2), (3, TOKENS, width))
    return base.astype(jnp.bfloat16)


def draw_clusters(key, part):
    return cluster_table(jax.random.fold_in(key, 11))


def block_levels(rng, shape, cuts, least, largest):
    gain, own = 1.0, jax.random.fold_in(rng, 6)
    for dim, shards_of in cuts:
        heights = jnp.exp(jax.random.uniform(jax.random.fold_in(own, dim), (shards_of,), jnp.float32, least / len(cuts), largest / len(cuts)))
        gain = gain * jnp.repeat(heights, shape[dim] // shards_of).reshape([-1 if axis == dim else 1 for axis in range(len(shape))])
    return gain


def centred(rng, dims, spread, most, cuts=(), kind=jnp.bfloat16):
    entries = jax.random.normal(rng, dims, jnp.float32) * spread
    if len(cuts) > 0:
        entries = block_levels(rng, dims, cuts, -0.22, 0.18) * entries
    return jnp.clip(entries, min=-most, max=most).astype(kind)


def setup_inputs(seed: int = 0) -> dict:
    streams_of = jax.random.split(jax.random.key(seed), 6)
    return {
        "local_qkv": draw_local_qkv(jax.random.fold_in(streams_of[5], 71), 0),
        "routed_qkv": draw_routed_qkv(jax.random.fold_in(streams_of[5], 71), 0),
        "clusters": draw_clusters(jax.random.fold_in(streams_of[5], 71), 0),
        "wo_local": centred(streams_of[3], (LOCAL_HEADS * DH, D), DH ** -0.5, 0.5, ((0, 4),)),
        "wo_routed": centred(streams_of[4], (ROUTED_HEADS * DH, D), DH ** -0.5, 0.5, ((0, 4),)),
    }


masked_fill = -1e30


def attend(scores, allowed, values, form):
    scores = jnp.where(allowed, scores, masked_fill)
    top_score = jnp.max(scores, axis=-1, keepdims=True)
    raised = jnp.exp(scores - top_score)
    weights = (raised / jnp.sum(raised, axis=-1, keepdims=True)).astype(jnp.bfloat16)
    weights = lax.optimization_barrier(weights)
    return jnp.einsum(form, weights.astype(jnp.float32), values.astype(jnp.float32)).astype(jnp.bfloat16)


def window_attend(qkv):
    width = qkv.shape[2]
    head_count = width // DH
    queries = qkv[0].reshape(TOKENS, head_count, DH)
    padded = jnp.concatenate([jnp.zeros((2, WINDOW, width), qkv.dtype), qkv[1:]], axis=1)

    def one_block(index):
        start = index * WINDOW
        block_q = lax.dynamic_slice_in_dim(queries, start, WINDOW, 0).astype(jnp.float32)
        block_kv = lax.dynamic_slice_in_dim(padded, start, 2 * WINDOW, 1).astype(jnp.float32)
        keys_here = block_kv[0].reshape(2 * WINDOW, head_count, DH)
        values_here = block_kv[1].reshape(2 * WINDOW, head_count, DH)
        scores = jnp.einsum("qhd,khd->hqk", block_q, keys_here) * (DH ** -0.5)
        query_at = start + jnp.arange(WINDOW, dtype=jnp.int32)
        key_at = start - WINDOW + jnp.arange(2 * WINDOW, dtype=jnp.int32)
        offset = key_at[None, :] - query_at[:, None]
        allowed = (offset <= 0) & (offset > -WINDOW) & (key_at[None, :] >= 0)
        return attend(scores, allowed[None], values_here, "hqk,khd->qhd").reshape(WINDOW, width)

    blocks = lax.map(one_block, jnp.arange(TOKENS // WINDOW, dtype=jnp.int32))
    return blocks.reshape(TOKENS, width)


def cluster_attend(qkv, table):
    head_count = table.shape[0]
    span = N_SEQ * MOST
    token_ids = jnp.arange(TOKENS, dtype=jnp.int32)

    def one_head(index):
        labels = table[index]
        order_index = jnp.argsort(labels * TOKENS + token_ids).astype(jnp.int32)
        head_rows = lax.dynamic_slice_in_dim(qkv, index * DH, DH, 2)
        sorted_rows = head_rows[:, order_index].astype(jnp.float32)
        sorted_labels = labels[order_index]
        padded_rows = jnp.concatenate([jnp.zeros((3, span, DH), jnp.float32), sorted_rows], axis=1)
        padded_labels = jnp.concatenate([jnp.full((span,), -1, jnp.int32), sorted_labels])
        padded_at = jnp.concatenate([jnp.full((span,), -1, jnp.int32), order_index])

        def one_block(block):
            start = block * span
            block_q = lax.dynamic_slice_in_dim(sorted_rows[0], start, span, 0)
            nearby = lax.dynamic_slice_in_dim(padded_rows, start, 2 * span, 1)
            query_label = lax.dynamic_slice_in_dim(sorted_labels, start, span, 0)
            query_at = lax.dynamic_slice_in_dim(order_index, start, span, 0)
            key_label = lax.dynamic_slice_in_dim(padded_labels, start, 2 * span, 0)
            key_at = lax.dynamic_slice_in_dim(padded_at, start, 2 * span, 0)
            scores = jnp.einsum("qd,kd->qk", block_q, nearby[1]) * (DH ** -0.5)
            allowed = (key_label[None, :] == query_label[:, None]) & (key_at[None, :] <= query_at[:, None])
            return attend(scores, allowed, nearby[2], "qk,kd->qd")

        outputs = lax.map(one_block, jnp.arange(TOKENS // span, dtype=jnp.int32)).reshape(TOKENS, DH)
        return jnp.zeros((TOKENS, DH), jnp.bfloat16).at[order_index].set(outputs)

    per_head = lax.map(one_head, jnp.arange(head_count, dtype=jnp.int32))
    return per_head.transpose(1, 0, 2).reshape(TOKENS, head_count * DH)


def reference(local_qkv, routed_qkv, clusters, wo_local, wo_routed):
    local_out = window_attend(local_qkv)
    routed_out = cluster_attend(routed_qkv, clusters)
    group_local = local_out.shape[1] // N_HEADS
    group_routed = routed_out.shape[1] // N_HEADS

    def one_rows(index):
        start = index * TOK_DEV
        rows_local = lax.dynamic_slice_in_dim(local_out, start, TOK_DEV, 0)
        rows_routed = lax.dynamic_slice_in_dim(routed_out, start, TOK_DEV, 0)
        total = jnp.zeros((TOK_DEV, D), jnp.float32)
        for group in range(N_HEADS):
            low_local = group * group_local
            low_routed = group * group_routed
            group_sum = jnp.dot(rows_local[:, low_local:low_local + group_local], wo_local[low_local:low_local + group_local], preferred_element_type=jnp.float32)
            group_sum = group_sum + jnp.dot(rows_routed[:, low_routed:low_routed + group_routed], wo_routed[low_routed:low_routed + group_routed], preferred_element_type=jnp.float32)
            total = total + lax.optimization_barrier(group_sum.astype(jnp.bfloat16)).astype(jnp.float32)
        return total.astype(jnp.bfloat16)

    layer_out = lax.map(one_rows, jnp.arange(TOKENS // TOK_DEV, dtype=jnp.int32))
    return layer_out.reshape(TOKENS, D)
```

```python
import functools
import math

import jax
import jax.numpy as jnp
from jax import lax
from jax.experimental import pallas as pl
from jax.experimental.pallas import tpu as pltpu
from jax.sharding import PartitionSpec as P

DH = 128
WINDOW = 512
MASKED = -1e30
SCALE2 = math.log2(math.e) / math.sqrt(DH)
VMEM_LIMIT = 56 << 20

NT = (((1,), (1,)), ((), ()))
MESH = pl.DeviceIdType.MESH


def vmem():
    return pl.BlockSpec(memory_space=pltpu.VMEM)


def dot_nt(a, b):
    return lax.dot_general(a, b, NT, preferred_element_type=jnp.float32)


def dot(a, b):
    return jnp.dot(a, b, preferred_element_type=jnp.float32)


def window_heads(is_first, own_ref, prev_ref, out_ref):
    tok_count, width = out_ref.shape
    rows = min(256, tok_count)
    span = rows + WINDOW
    for i in range(tok_count // rows):
        r = lax.broadcasted_iota(jnp.int32, (rows, span), 0)
        c = lax.broadcasted_iota(jnp.int32, (rows, span), 1)
        from_prev = WINDOW - i * rows
        lowest = jnp.where(is_first, from_prev, 0)
        allowed = (c > r) & (c <= r + WINDOW) & (c >= lowest)
        for h in range(width // DH):
            cols = slice(h * DH, (h + 1) * DH)
            q = own_ref[0, i * rows:(i + 1) * rows, cols]
            k = jnp.concatenate(
                [prev_ref[0, i * rows:, cols], own_ref[1, :(i + 1) * rows, cols]], axis=0)
            v = jnp.concatenate(
                [prev_ref[1, i * rows:, cols], own_ref[2, :(i + 1) * rows, cols]], axis=0)
            s = jnp.where(allowed, dot_nt(q, k), MASKED)
            top = jnp.max(s, axis=-1, keepdims=True)
            p = jnp.exp2((s - top) * SCALE2)
            total = jnp.sum(p, axis=-1, keepdims=True)
            o = dot(p.astype(jnp.bfloat16), v) / total
            out_ref[i * rows:(i + 1) * rows, cols] = o.astype(jnp.bfloat16)


def flipped(me, t, n):
    out = 0
    bit = 1
    while bit < n:
        out = out + lax.rem(lax.div(me, bit) + lax.div(jnp.int32(t), bit), 2) * bit
        bit *= 2
    return out


def layer_kernel(n, heads, qkv_ref, id_ref, local_ref, wl_any, wr_any, out_ref, prev, rq, kv, ck, cq, acc, top, total, done,
                   own_sem, q_sem, kv_sem, id_sem, pass_sem, back_sem, prev_sem,
                 local_out, x, wl, wr, tiles_out, tiles_in, out_sem, in_sem, w_sem):
    group = n // heads
    tok_count = x.shape[0]
    rows = tok_count // group
    tile = min(256, tok_count)
    me = lax.axis_index("seq")
    head = lax.div(me, group)
    part = lax.rem(me, group)

    def rows_of(p):
        return pl.ds(pl.multiple_of(p * rows, rows), rows)

    def remote(src, dst, sem, index, device):
        return pltpu.make_async_remote_copy(
            src_ref=src, dst_ref=dst, send_sem=sem.at[(0,) + index], recv_sem=sem.at[(1,) + index],
            device_id={"seq": device}, device_id_type=MESH)

    def copies(t):
        d = flipped(me, t, n)
        h = pl.ds(pl.multiple_of(lax.div(d, group) * DH, DH), DH)
        p = rows_of(lax.rem(d, group))
        return (
            remote(id_ref.at[lax.div(d, group)], ck.at[me], id_sem, (t,), d),
            remote(qkv_ref.at[pl.ds(1, 2), p, h], kv.at[me, :, p], kv_sem, (t,), d),
            remote(qkv_ref.at[0, p, h], rq.at[me], q_sem, (t,), d),
        )

    def passed(u, g):
        src = kv.at[pl.ds(flipped(head, u, heads) * group, group), :, rows_of(part)]
        return remote(src, src, pass_sem, (u, g - 1), flipped(me, g, n))

    barrier = pltpu.get_barrier_semaphore()

    def greet(t, _):
        pl.semaphore_signal(barrier, inc=1, device_id={"seq": flipped(me, t, n)},
                            device_id_type=MESH)
        return 0

    lax.fori_loop(1, n, greet, 0)
    place = lax.axis_index("heads")
    across = (place + 1 - 2 * lax.rem(place, 2), lax.rem(place + 2, 4))
    for device in across:
        pl.semaphore_signal(barrier, inc=1, device_id={"heads": device}, device_id_type=MESH)
    weights = (
        pltpu.make_async_copy(wl_any, wl, w_sem.at[0]),
        pltpu.make_async_copy(wr_any, wr, w_sem.at[1]),
    )
    my_cols = pl.ds(pl.multiple_of(head * DH, DH), DH)
    own = (
        pltpu.make_async_copy(id_ref.at[head], ck.at[me], own_sem.at[0]),
        pltpu.make_async_copy(qkv_ref.at[pl.ds(1, 2), rows_of(part), my_cols],
                              kv.at[me, :, rows_of(part)], own_sem.at[1]),
        pltpu.make_async_copy(qkv_ref.at[0, rows_of(part), my_cols], rq.at[me], own_sem.at[2]),
    )
    for copy in own:
        copy.start()
    pl.semaphore_wait(barrier, n - 1 + len(across))

    def send(t, _):
        for copy in copies(t):
            copy.start()
        return 0

    lax.fori_loop(1, n, send, 0)
    for copy in weights:
        copy.start()
    prev_copy = remote(local_ref.at[pl.ds(1, 2)], prev, prev_sem, (), lax.rem(me + 1, n))

    @pl.when(me < n - 1)
    def _():
        prev_copy.start()

    @pl.when(me == 0)
    def _():
        prev[...] = jnp.zeros_like(prev)

    def update(qg, kg, c, r, diagonal):
        blocks = min(2, group)
        if diagonal and group == 2 and rows == tile:
            blocks = r + 1
        span = blocks * tok_count
        at = slice(r * tile, (r + 1) * tile)
        first = kg * group + c * 2
        per = tile // rows
        q = rq[pl.ds(qg * group + r * per, per)].reshape(tile, DH)
        k = kv[pl.ds(first, blocks), 0].reshape(span, DH)
        v = kv[pl.ds(first, blocks), 1].reshape(span, DH)
        ids = jnp.concatenate([ck[first + i] for i in range(blocks)], axis=1)
        allowed = cq[qg, at, :1] == ids.astype(jnp.float32)
        if diagonal:
            i = r * tile + lax.broadcasted_iota(jnp.int32, (tile, 1), 0)
            shift = rows.bit_length() - 1
            place = (i >> shift) * tok_count + part * rows + (i & (rows - 1))
            key = c * 2 * tok_count + lax.broadcasted_iota(jnp.int32, (1, span), 1)
            allowed = allowed & (key <= place)
        s = jnp.where(allowed, dot_nt(q, k), MASKED)
        old = top[qg, at]
        new = jnp.maximum(old, jnp.max(s, axis=-1, keepdims=True))
        fade = jnp.exp2((old - new) * SCALE2)
        p = jnp.exp2((s - new) * SCALE2)
        top[qg, at] = new
        total[qg, at] = fade * total[qg, at] + jnp.sum(p, axis=-1, keepdims=True)
        acc[qg, at] = fade * acc[qg, at] + dot(p.astype(jnp.bfloat16), v)

    def updates(qg, kg, diagonal):
        def chunk(c, _):
            for r in range(tok_count // tile):
                update(qg, kg, c, r, diagonal)
            return 0

        if group <= 2:
            chunk(0, 0)
        else:
            lax.fori_loop(0, group // 2, chunk, 0)

    def back(t):
        d = flipped(me, t, n)
        return remote(done.at[d], x.at[rows_of(part), my_cols], back_sem, (t,), d)

    own_back = pltpu.make_async_copy(done.at[me], x.at[rows_of(part), my_cols], own_sem.at[3])

    def finish(v):
        g = flipped(head, v, heads)
        o = (acc[g] / total[g]).astype(jnp.bfloat16)
        done[pl.ds(g * group, group)] = o.reshape(group, rows, DH)
        if v == 0:
            own_back.start()

        def give(t, _):
            back(t).start()
            return 0

        lax.fori_loop(max(v * group, 1), (v + 1) * group, give, 0)

    for u in range(heads):
        if u == 0:
            for copy in own:
                copy.wait()

        def arrive(t, _):
            for copy in copies(t):
                copy.wait_recv()
            return 0

        lax.fori_loop(max(u * group, 1), (u + 1) * group, arrive, 0)
        for g in range(1, group):
            passed(u, g).start()
        a = flipped(head, u, heads)

        def prepare(w, _):
            row = ck[a * group + w].astype(jnp.float32)
            column = jnp.transpose(jnp.broadcast_to(row, (128, tok_count)))
            done_rows = pl.ds(pl.multiple_of(w * rows, rows), rows)
            acc[a] = column
            cq[a, done_rows] = acc[a, rows_of(part)]
            return 0

        lax.fori_loop(0, group, prepare, 0)
        top[a] = jnp.full(top.shape[1:], MASKED, jnp.float32)
        total[a] = jnp.zeros(total.shape[1:], jnp.float32)
        acc[a] = jnp.zeros(acc.shape[1:], jnp.float32)
        for g in range(1, group):
            passed(u, g).wait_recv()
        updates(a, a, True)
        for v in reversed(range(u)):
            b = flipped(head, v, heads)
            updates(jnp.maximum(a, b), jnp.minimum(a, b), False)
            if u == heads - 1:
                finish(v)
    finish(heads - 1)

    @pl.when(me > 0)
    def _():
        prev_copy.wait_recv()

    window_heads(me == 0, local_ref, prev, local_out)

    @pl.when(me < n - 1)
    def _():
        prev_copy.wait_send()

    def settle(t, _):
        for copy in copies(t):
            copy.wait_send()
        back(t).wait()
        return 0

    lax.fori_loop(1, n, settle, 0)
    own_back.wait()
    for u in range(heads):
        for g in range(1, group):
            passed(u, g).wait_send()
    for copy in weights:
        copy.wait()
    project(place, across, local_out, x, wl, wr, out_ref, tiles_out, tiles_in, out_sem, in_sem)


def project(me, across, local_ref, x, wl_ref, wr_ref, out_ref, send, recv, send_sem, recv_sem):
    cols = out_ref.shape[1]
    pieces = send.shape[1]
    tile = cols // pieces
    corner = lax.rem(across[0] + 2, 4)

    def product(owner, c):
        at = pl.ds(pl.multiple_of(owner * cols + c * tile, tile), tile)
        return dot(local_ref[...], wl_ref[:, at]) + dot(x[...], wr_ref[:, at])

    def hand(kind, c, value, device):
        send[kind, c] = value.astype(jnp.bfloat16)
        return pltpu.make_async_remote_copy(
            src_ref=send.at[kind, c], dst_ref=recv.at[kind, c],
            send_sem=send_sem.at[kind, c], recv_sem=recv_sem.at[kind, c],
            device_id={"heads": device}, device_id_type=MESH)

    order = [c + half * (pieces // 2) for c in range(pieces // 2) for half in range(2)]
    way = [c // (pieces // 2) for c in range(pieces)]
    copies = {}
    for kind in range(2):
        for c in order:
            device = across[way[c]]
            copies[kind, c] = hand(kind, c, product(device if kind else corner, c), device)
            copies[kind, c].start()
    for c in order:
        device = across[1 - way[c]]
        value = product(device, c)
        copies[0, c].wait_recv()
        copies[2, c] = hand(2, c, value + recv[0, c].astype(jnp.float32), device)
        copies[2, c].start()
    for c in order:
        value = product(me, c)
        copies[1, c].wait_recv()
        value = value + recv[1, c].astype(jnp.float32)
        copies[2, c].wait_recv()
        value = value + recv[2, c].astype(jnp.float32)
        out_ref[:, c * tile:(c + 1) * tile] = value.astype(jnp.bfloat16)
    for copy in copies.values():
        copy.wait_send()


def body(local_qkv, routed_qkv, clusters, wo_local, wo_routed):
    tok_count = routed_qkv.shape[1]
    heads = clusters.shape[0]
    n = lax.axis_size("seq")
    group = n // heads
    rows = tok_count // group
    cols = wo_local.shape[1] // lax.axis_size("heads")
    slots = (3, 4, tok_count, cols // 4)
    DMA = pltpu.SemaphoreType.DMA
    return pl.pallas_call(
        functools.partial(layer_kernel, n, heads),
        out_shape=jax.ShapeDtypeStruct((tok_count, cols), jnp.bfloat16),
        in_specs=[vmem()] * 3 + [pl.BlockSpec(memory_space=pl.ANY)] * 2,
        out_specs=vmem(),
        scratch_shapes=[
            pltpu.VMEM((2,) + local_qkv.shape[1:], jnp.bfloat16),
            pltpu.VMEM((n, rows, DH), jnp.bfloat16),
            pltpu.VMEM((n, 2, tok_count, DH), jnp.bfloat16),
            pltpu.VMEM((n, 1, tok_count), jnp.int32),
            pltpu.VMEM((heads, tok_count, 128), jnp.float32),
            pltpu.VMEM((heads, tok_count, DH), jnp.float32),
            pltpu.VMEM((heads, tok_count, 1), jnp.float32),
            pltpu.VMEM((heads, tok_count, 1), jnp.float32),
            pltpu.VMEM((n, rows, DH), jnp.bfloat16),
            DMA((4,)), DMA((2, n)), DMA((2, n)), DMA((2, n)),
            DMA((2, heads, max(group - 1, 1))), DMA((2, n)), DMA((2,)),
            pltpu.VMEM(local_qkv.shape[1:], jnp.bfloat16),
            pltpu.VMEM((tok_count, heads * DH), jnp.bfloat16),
            pltpu.VMEM(wo_local.shape, jnp.bfloat16),
            pltpu.VMEM(wo_routed.shape, jnp.bfloat16),
            pltpu.VMEM(slots, jnp.bfloat16),
            pltpu.VMEM(slots, jnp.bfloat16),
            DMA(slots[:2]), DMA(slots[:2]), DMA((2,)),
        ],
        cost_estimate=pl.CostEstimate(
            flops=4 << 30, bytes_accessed=200 << 20, transcendentals=8 << 20),
        compiler_params=pltpu.CompilerParams(
            vmem_limit_bytes=VMEM_LIMIT, collective_id=0, has_side_effects=True),
    )(routed_qkv, clusters.reshape(heads, 1, tok_count), local_qkv, wo_local, wo_routed)


ROUNDS = 4
LAG = 2
CLUSTERS = 128


def chain_kernel(n, routed, ids, local, wl_any, wr_any, out_ref,
                 kaug, vaug, q_own, qbuf, qmask, id_key, id_query, opart, spart, osend, orecv, ssend, srecv,
                 lq, lkv, lout, x, wl, wr, rsend, rrecv,
                 load_sem, key_sem, kid_sem, q_sem, qid_sem, o_sem, s_sem, halo_sem, w_sem, r_sem):
    chips = n // 2
    tok = q_own.shape[0]
    width = q_own.shape[1]
    heads = width // DH
    rounds = o_sem.shape[2]
    rows = tok // rounds
    cols = out_ref.shape[1]
    half_cols = cols // 2
    me = lax.axis_index("seq")
    z = lax.div(me, 2)
    core = lax.rem(me, 2)
    partner = me + 1 - 2 * core
    place = lax.axis_index("heads")
    across = (place + 1 - 2 * lax.rem(place, 2), lax.rem(place + 2, 4))
    corner = lax.rem(across[0] + 2, 4)

    def at(r):
        return pl.ds(pl.multiple_of(r * rows, rows), rows)

    def remote(src, dst, sem, index, **device):
        return pltpu.make_async_remote_copy(
            src_ref=src, dst_ref=dst, send_sem=sem.at[(0,) + index], recv_sem=sem.at[(1,) + index],
            device_id=device, device_id_type=MESH)

    barrier = pltpu.get_barrier_semaphore()
    greeted = jnp.int32(len(across))
    for d in (-2, -1, 1, 2):
        there = (me + d >= 0) & (me + d < n)

        @pl.when(there)
        def _():
            pl.semaphore_signal(barrier, inc=1, device_id={"seq": me + d}, device_id_type=MESH)

        greeted = greeted + there.astype(jnp.int32)
    for device in across:
        pl.semaphore_signal(barrier, inc=1, device_id={"heads": device}, device_id_type=MESH)

    mine = pl.ds(pl.multiple_of(core * tok, tok), tok)
    loads = []
    for i, aug in enumerate((kaug, vaug)):
        for h in range(heads):
            loads.append((routed.at[1 + i, :, h * DH:(h + 1) * DH], aug.at[h, mine, pl.ds(0, DH)]))
    loads.append((routed.at[0], q_own))
    loads.append((ids, id_key.at[core]))
    loads.append((local.at[0], lq))
    loads.append((local.at[pl.ds(1, 2)], lkv.at[:, pl.ds(tok, tok)]))
    loads = [pltpu.make_async_copy(a, b, load_sem.at[i]) for i, (a, b) in enumerate(loads)]
    for copy in loads:
        copy.start()

    keys = [remote(routed.at[1 + i, :, h * DH:(h + 1) * DH], aug.at[h, mine, pl.ds(0, DH)], key_sem, (i, h),
                   seq=partner)
            for h in range(heads) for i, aug in enumerate((kaug, vaug))]
    keys.append(remote(ids, id_key.at[core], kid_sem, (), seq=partner))
    halo = remote(local.at[pl.ds(1, 2)], lkv.at[:, pl.ds(0, tok)], halo_sem, (), seq=me + 1)
    weights = (
        pltpu.make_async_copy(wl_any, wl, w_sem.at[0]),
        pltpu.make_async_copy(wr_any, wr, w_sem.at[1]),
    )

    def q_copy(j, r, src=None):
        slot = qbuf.at[j - 1, at(r)]
        return remote(slot if src is None else src, slot, q_sem, (j - 1, r), seq=me - 2)

    def qid_copy(j, src=None):
        slot = id_query.at[j - 1]
        return remote(slot if src is None else src, slot, qid_sem, (j - 1,), seq=me - 2)

    def own_q(r):
        return q_copy(z, r, routed.at[0, at(r)])

    def o_copies(j, r):
        return (
            remote(osend.at[j - 1, at(r)], orecv.at[j - 1, at(r)], o_sem, (j - 1, r), seq=me + 2),
            remote(ssend.at[j - 1, r], srecv.at[j - 1, r], s_sem, (j - 1, r), seq=me + 2),
        )

    def r_copy(kind, r, half):
        device = across[half] if kind < 2 else across[1 - half]
        return remote(rsend.at[kind, r, half], rrecv.at[kind, r, half], r_sem, (kind, r, half), heads=device)

    pl.semaphore_wait(barrier, greeted)

    @pl.when(z > 0)
    def _():
        qid_copy(z, ids).start()
        own_q(0).start()

    for copy in keys:
        copy.start()

    @pl.when(me < n - 1)
    def _():
        halo.start()

    for copy in weights:
        copy.start()

    def table(row, on, off):
        c = lax.broadcasted_iota(jnp.int32, (CLUSTERS, tok), 0)
        t = jnp.where(c == row, jnp.float32(on), jnp.float32(off))
        return jnp.transpose(t).astype(jnp.bfloat16)

    def mask_of(slot, id_ref):
        for h in range(heads):
            qmask[slot, h] = table(id_ref[h:h + 1, :], 0.0, MASKED)

    def key_table(c):
        where = pl.ds(pl.multiple_of(c * tok, tok), tok)
        for h in range(heads):
            kaug[h, where, DH:] = table(id_key[c, h:h + 1, :], 1.0, 0.0)

    for h in range(heads):
        vaug[h, :, DH:] = jnp.ones((2 * tok, DH), jnp.bfloat16)

    @pl.when(me == 0)
    def _():
        lkv[:, :tok] = jnp.zeros((2, tok, width), jnp.bfloat16)

    mask_of(0, ids)
    for copy in loads:
        copy.wait()
    key_table(core)
    for copy in keys:
        copy.wait_recv()
    key_table(1 - core)

    lane = lax.broadcasted_iota(jnp.int32, (1, DH), 1)

    def softmax(h, q, masks, allowed):
        s = dot_nt(jnp.concatenate([q, masks], axis=1), kaug[h])
        if allowed is not None:
            s = jnp.where(allowed, s, MASKED)
        top = jnp.max(s, axis=-1, keepdims=True)
        p = jnp.exp2((s - top) * SCALE2).astype(jnp.bfloat16)
        o = dot(p, vaug[h])
        total = o[:, DH:]
        return o[:, :DH] / total, top * SCALE2 + jnp.log2(total)

    def attend_own(r):
        i = core * tok + r * rows + lax.broadcasted_iota(jnp.int32, (rows, 1), 0)
        allowed = lax.broadcasted_iota(jnp.int32, (1, 2 * tok), 1) <= i

        def head(h, stat):
            hc = pl.ds(pl.multiple_of(h * DH, DH), DH)
            o, level = softmax(h, q_own[at(r), hc], qmask[0, h, at(r)], allowed)
            opart[0, at(r), hc] = o
            return jnp.where(lane == h, level, stat)

        spart[0, at(r)] = lax.fori_loop(0, heads, head, jnp.zeros((rows, DH), jnp.float32), unroll=True)

    def attend(first, r):
        count = chips - first
        spart[pl.ds(first, count), at(r)] = jnp.zeros((count, rows, DH), jnp.float32)

        def head(h, _):
            hc = pl.ds(pl.multiple_of(h * DH, DH), DH)
            q = qbuf[first - 1:, at(r), hc].reshape(count * rows, DH)
            masks = qmask[first:, h, at(r)].reshape(count * rows, DH)
            o, level = softmax(h, q, masks, None)
            if first == 1:
                osend[:, at(r), hc] = o.astype(jnp.bfloat16).reshape(count, rows, DH)
            else:
                opart[first:, at(r), hc] = o.reshape(count, rows, DH)
            old = spart[first:, at(r)]
            spart[first:, at(r)] = jnp.where(lane == h, level.reshape(count, rows, DH), old)
            return 0

        lax.fori_loop(0, heads, head, 0, unroll=True)

    def window(r):
        i = lax.broadcasted_iota(jnp.int32, (rows, rows + WINDOW), 0)
        c = lax.broadcasted_iota(jnp.int32, (rows, rows + WINDOW), 1)
        lowest = jnp.where(me == 0, WINDOW - r * rows, 0)
        allowed = (c > i) & (c <= i + WINDOW) & (c >= lowest)
        span = pl.ds(pl.multiple_of(r * rows, rows), rows + WINDOW)

        def head(h, _):
            hc = pl.ds(pl.multiple_of(h * DH, DH), DH)
            s = jnp.where(allowed, dot_nt(lq[at(r), hc], lkv[0, span, hc]), MASKED)
            top = jnp.max(s, axis=-1, keepdims=True)
            p = jnp.exp2((s - top) * SCALE2)
            total = jnp.sum(p, axis=-1, keepdims=True)
            o = dot(p.astype(jnp.bfloat16), lkv[1, span, hc]) / total
            lout[at(r), hc] = o.astype(jnp.bfloat16)
            return 0

        lax.fori_loop(0, heads, head, 0, unroll=True)

    def send_stat(j, r, level):
        ssend[j - 1, r] = jnp.transpose(level)[:8]

    def merge(j, r, slot, last):
        for copy in o_copies(j, r):
            copy.wait_recv()
        level_in = jnp.transpose(jnp.concatenate(
            [srecv[j - 1, r], jnp.zeros((DH - 8, rows), jnp.float32)], axis=0))
        level_own = spart[slot, at(r)]
        high = jnp.maximum(level_in, level_own)
        w_in = jnp.exp2(level_in - high)
        w_own = jnp.exp2(level_own - high)
        total = w_in + w_own
        w_in = w_in / total
        w_own = w_own / total
        for h in range(heads):
            hc = slice(h * DH, (h + 1) * DH)
            o = w_in[:, h:h + 1] * orecv[j - 1, at(r), hc].astype(jnp.float32) + w_own[:, h:h + 1] * opart[slot, at(r), hc]
            if last:
                x[at(r), hc] = o.astype(jnp.bfloat16)
            else:
                osend[j - 1, at(r), hc] = o.astype(jnp.bfloat16)
        if not last:
            send_stat(j, r, high + jnp.log2(total))
            for copy in o_copies(j, r):
                copy.start()

    def product(owner, half, r):
        c = pl.ds(pl.multiple_of(owner * cols + half * half_cols, half_cols), half_cols)
        return dot(lout[at(r)], wl[:, c]) + dot(x[at(r)], wr[:, c])

    def hand(kind, r, half, value):
        rsend[kind, r, half] = value.astype(jnp.bfloat16)
        r_copy(kind, r, half).start()

    def reduce1(r):
        for half in range(2):
            hand(0, r, half, product(corner, half, r))
        for half in range(2):
            hand(1, r, half, product(across[half], half, r))

    def reduce2(r):
        for half in range(2):
            value = product(across[1 - half], half, r)
            r_copy(0, r, half).wait_recv()
            hand(2, r, half, value + rrecv[0, r, half].astype(jnp.float32))

    def reduce3(r):
        for half in range(2):
            value = product(place, half, r)
            for kind in (1, 2):
                r_copy(kind, r, half).wait_recv()
                value = value + rrecv[kind, r, half].astype(jnp.float32)
            out_ref[at(r), half * half_cols:(half + 1) * half_cols] = value.astype(jnp.bfloat16)

    def guarded(cond, f, *args):
        @pl.when(cond)
        def _():
            f(*args)

    @pl.when(z == 0)
    def _():
        @pl.when(me > 0)
        def _():
            halo.wait_recv()

        for copy in weights:
            copy.wait()

        def step(t, _):
            @pl.when(t < rounds)
            def _():
                attend_own(t)
                for h in range(heads):
                    hc = slice(h * DH, (h + 1) * DH)
                    x[at(t), hc] = opart[0, at(t), hc].astype(jnp.bfloat16)
                window(t)
                reduce1(t)

                @pl.when(t == 0)
                def _():
                    for j in range(1, chips):
                        qid_copy(j).wait_recv()
                        mask_of(j, id_query.at[j - 1])

                for j in range(1, chips):
                    q_copy(j, t).wait_recv()
                attend(1, t)
                for j in range(1, chips):
                    send_stat(j, t, spart[j, at(t)])
                    for copy in o_copies(j, t):
                        copy.start()

            guarded((t >= 1) & (t <= rounds), lambda: reduce2(t - 1))
            guarded(t >= 2, lambda: reduce3(t - 2))
            return 0

        lax.fori_loop(0, rounds + 2, step, 0)

    @pl.when(z > 0)
    def _():
        def step(t, _):
            @pl.when(t < rounds)
            def _():
                for j in range(2, chips):
                    @pl.when(z < j)
                    def _():
                        @pl.when(t == 0)
                        def _():
                            qid_copy(j).wait_recv()
                            qid_copy(j).start()
                        q_copy(j, t).wait_recv()
                        q_copy(j, t).start()

                @pl.when(t < rounds - 1)
                def _():
                    own_q(t + 1).start()

                @pl.when(t == 0)
                def _():
                    for j in range(2, chips):
                        guarded(z < j, mask_of, j, id_query.at[j - 1])

                for first in range(2, chips):
                    guarded(z == first - 1, attend, first, t)
                attend_own(t)

            @pl.when(t == 1)
            def _():
                halo.wait_recv()
                for copy in weights:
                    copy.wait()

            guarded((t >= 1) & (t <= rounds), lambda: window(t - 1))

            @pl.when((t >= LAG) & (t < rounds + LAG))
            def _():
                r = t - LAG
                for j in range(1, chips):
                    guarded(z == j, merge, j, r, 0, True)
                for j in range(2, chips):
                    guarded(z < j, merge, j, r, j, False)
                reduce1(r)

            guarded((t >= LAG + 1) & (t < rounds + LAG + 1), lambda: reduce2(t - LAG - 1))
            guarded(t >= LAG + 2, lambda: reduce3(t - LAG - 2))
            return 0

        lax.fori_loop(0, rounds + LAG + 2, step, 0)

    for copy in keys:
        copy.wait_send()
    guarded(me < n - 1, halo.wait_send)

    def settle(r, _):
        for j in range(1, chips):
            @pl.when((z > 0) & (z <= j))
            def _():
                q_copy(j, r).wait_send()

            @pl.when(z < j)
            def _():
                for copy in o_copies(j, r):
                    copy.wait_send()
        for kind in range(3):
            for half in range(2):
                r_copy(kind, r, half).wait_send()
        return 0

    lax.fori_loop(0, rounds, settle, 0)
    for j in range(1, chips):
        @pl.when((z > 0) & (z <= j))
        def _():
            qid_copy(j).wait_send()


def chain_body(local_qkv, routed_qkv, clusters, wo_local, wo_routed):
    tok, width = routed_qkv.shape[1:]
    heads = clusters.shape[0]
    n = lax.axis_size("seq")
    chips = n // 2
    rows = tok // ROUNDS
    cols = wo_local.shape[1] // lax.axis_size("heads")
    DMA = pltpu.SemaphoreType.DMA
    any_spec = pl.BlockSpec(memory_space=pl.ANY)

    def bf16(*shape):
        return pltpu.VMEM(shape, jnp.bfloat16)

    def f32(*shape):
        return pltpu.VMEM(shape, jnp.float32)

    slots = (3, ROUNDS, 2, rows, cols // 2)
    return pl.pallas_call(
        functools.partial(chain_kernel, n),
        out_shape=jax.ShapeDtypeStruct((tok, cols), jnp.bfloat16),
        in_specs=[any_spec, vmem(), any_spec, any_spec, any_spec],
        out_specs=vmem(),
        scratch_shapes=[
            bf16(heads, 2 * tok, 2 * DH), bf16(heads, 2 * tok, 2 * DH),
            bf16(tok, width), bf16(chips - 1, tok, width), bf16(chips, heads, tok, CLUSTERS),
            pltpu.VMEM((2, heads, tok), jnp.int32), pltpu.VMEM((chips - 1, heads, tok), jnp.int32),
            f32(chips, tok, width), f32(chips, tok, DH),
            bf16(chips - 1, tok, width), bf16(chips - 1, tok, width),
            f32(chips - 1, ROUNDS, 8, rows), f32(chips - 1, ROUNDS, 8, rows),
            bf16(tok, width), bf16(2, 2 * tok, width), bf16(tok, width), bf16(tok, width),
            bf16(*wo_local.shape), bf16(*wo_routed.shape), bf16(*slots), bf16(*slots),
            DMA((2 * heads + 4,)), DMA((2, 2, heads)), DMA((2,)),
            DMA((2, chips - 1, ROUNDS)), DMA((2, chips - 1)),
            DMA((2, chips - 1, ROUNDS)), DMA((2, chips - 1, ROUNDS)),
            DMA((2,)), DMA((2,)), DMA((2,) + slots[:3]),
        ],
        cost_estimate=pl.CostEstimate(
            flops=8 << 30, bytes_accessed=20 << 20, transcendentals=8 << 20),
        compiler_params=pltpu.CompilerParams(
            vmem_limit_bytes=VMEM_LIMIT, collective_id=1, has_side_effects=True),
    )(routed_qkv, clusters, local_qkv, wo_local, wo_routed)


def solution(mesh):
    return jax.shard_map(
        chain_body if mesh.shape["seq"] <= 8 else body,
        mesh=mesh,
        in_specs=(
            P(None, "seq", "heads"),
            P(None, "seq", "heads"),
            P("heads", "seq"),
            P("heads", None),
            P("heads", None),
        ),
        out_specs=P("seq", "heads"),
        check_vma=False,
    )
```

```python
import functools
import math

import jax
import jax.numpy as jnp
from jax import lax
from jax.experimental import pallas as pl
from jax.experimental.pallas import tpu as pltpu
from jax.sharding import PartitionSpec as P

DH = 128
WINDOW = 512
MASKED = -1e30
SCALE2 = math.log2(math.e) / math.sqrt(DH)
VMEM_LIMIT = 56 << 20

NT = (((1,), (1,)), ((), ()))
MESH = pl.DeviceIdType.MESH


def vmem():
    return pl.BlockSpec(memory_space=pltpu.VMEM)


def dot_nt(a, b):
    return lax.dot_general(a, b, NT, preferred_element_type=jnp.float32)


def dot(a, b):
    return jnp.dot(a, b, preferred_element_type=jnp.float32)


def window_heads(is_first, own_ref, prev_ref, out_ref):
    tok_count, width = out_ref.shape
    rows = min(256, tok_count)
    span = rows + WINDOW
    for i in range(tok_count // rows):
        r = lax.broadcasted_iota(jnp.int32, (rows, span), 0)
        c = lax.broadcasted_iota(jnp.int32, (rows, span), 1)
        from_prev = WINDOW - i * rows
        lowest = jnp.where(is_first, from_prev, 0)
        allowed = (c > r) & (c <= r + WINDOW) & (c >= lowest)
        for h in range(width // DH):
            cols = slice(h * DH, (h + 1) * DH)
            q = own_ref[0, i * rows:(i + 1) * rows, cols]
            k = jnp.concatenate(
                [prev_ref[0, i * rows:, cols], own_ref[1, :(i + 1) * rows, cols]], axis=0)
            v = jnp.concatenate(
                [prev_ref[1, i * rows:, cols], own_ref[2, :(i + 1) * rows, cols]], axis=0)
            s = jnp.where(allowed, dot_nt(q, k), MASKED)
            top = jnp.max(s, axis=-1, keepdims=True)
            p = jnp.exp2((s - top) * SCALE2)
            total = jnp.sum(p, axis=-1, keepdims=True)
            o = dot(p.astype(jnp.bfloat16), v) / total
            out_ref[i * rows:(i + 1) * rows, cols] = o.astype(jnp.bfloat16)


def flipped(me, t, n):
    out = 0
    bit = 1
    while bit < n:
        out = out + lax.rem(lax.div(me, bit) + lax.div(jnp.int32(t), bit), 2) * bit
        bit *= 2
    return out


def layer_kernel(n, heads, qkv_ref, id_ref, local_ref, wl_any, wr_any, out_ref, prev, rq, kv, ck, cq, acc, top, total, done,
                   own_sem, q_sem, kv_sem, id_sem, pass_sem, back_sem, prev_sem,
                 local_out, x, wl, wr, tiles_out, tiles_in, out_sem, in_sem, w_sem):
    group = n // heads
    tok_count = x.shape[0]
    rows = tok_count // group
    tile = min(256, tok_count)
    me = lax.axis_index("seq")
    head = lax.div(me, group)
    part = lax.rem(me, group)

    def rows_of(p):
        return pl.ds(pl.multiple_of(p * rows, rows), rows)

    def remote(src, dst, sem, index, device):
        return pltpu.make_async_remote_copy(
            src_ref=src, dst_ref=dst, send_sem=sem.at[(0,) + index], recv_sem=sem.at[(1,) + index],
            device_id={"seq": device}, device_id_type=MESH)

    def copies(t):
        d = flipped(me, t, n)
        h = pl.ds(pl.multiple_of(lax.div(d, group) * DH, DH), DH)
        p = rows_of(lax.rem(d, group))
        return (
            remote(id_ref.at[lax.div(d, group)], ck.at[me], id_sem, (t,), d),
            remote(qkv_ref.at[pl.ds(1, 2), p, h], kv.at[me, :, p], kv_sem, (t,), d),
            remote(qkv_ref.at[0, p, h], rq.at[me], q_sem, (t,), d),
        )

    def passed(u, g):
        src = kv.at[pl.ds(flipped(head, u, heads) * group, group), :, rows_of(part)]
        return remote(src, src, pass_sem, (u, g - 1), flipped(me, g, n))

    barrier = pltpu.get_barrier_semaphore()

    def greet(t, _):
        pl.semaphore_signal(barrier, inc=1, device_id={"seq": flipped(me, t, n)},
                            device_id_type=MESH)
        return 0

    lax.fori_loop(1, n, greet, 0)
    place = lax.axis_index("heads")
    across = (place + 1 - 2 * lax.rem(place, 2), lax.rem(place + 2, 4))
    for device in across:
        pl.semaphore_signal(barrier, inc=1, device_id={"heads": device}, device_id_type=MESH)
    weights = (
        pltpu.make_async_copy(wl_any, wl, w_sem.at[0]),
        pltpu.make_async_copy(wr_any, wr, w_sem.at[1]),
    )
    my_cols = pl.ds(pl.multiple_of(head * DH, DH), DH)
    own = (
        pltpu.make_async_copy(id_ref.at[head], ck.at[me], own_sem.at[0]),
        pltpu.make_async_copy(qkv_ref.at[pl.ds(1, 2), rows_of(part), my_cols],
                              kv.at[me, :, rows_of(part)], own_sem.at[1]),
        pltpu.make_async_copy(qkv_ref.at[0, rows_of(part), my_cols], rq.at[me], own_sem.at[2]),
    )
    for copy in own:
        copy.start()
    pl.semaphore_wait(barrier, n - 1 + len(across))

    def send(t, _):
        for copy in copies(t):
            copy.start()
        return 0

    lax.fori_loop(1, n, send, 0)
    for copy in weights:
        copy.start()
    prev_copy = remote(local_ref.at[pl.ds(1, 2)], prev, prev_sem, (), lax.rem(me + 1, n))

    @pl.when(me < n - 1)
    def _():
        prev_copy.start()

    @pl.when(me == 0)
    def _():
        prev[...] = jnp.zeros_like(prev)

    def update(qg, kg, c, r, diagonal):
        blocks = min(2, group)
        if diagonal and group == 2 and rows == tile:
            blocks = r + 1
        span = blocks * tok_count
        at = slice(r * tile, (r + 1) * tile)
        first = kg * group + c * 2
        per = tile // rows
        q = rq[pl.ds(qg * group + r * per, per)].reshape(tile, DH)
        k = kv[pl.ds(first, blocks), 0].reshape(span, DH)
        v = kv[pl.ds(first, blocks), 1].reshape(span, DH)
        ids = jnp.concatenate([ck[first + i] for i in range(blocks)], axis=1)
        allowed = cq[qg, at, :1] == ids.astype(jnp.float32)
        if diagonal:
            i = r * tile + lax.broadcasted_iota(jnp.int32, (tile, 1), 0)
            shift = rows.bit_length() - 1
            place = (i >> shift) * tok_count + part * rows + (i & (rows - 1))
            key = c * 2 * tok_count + lax.broadcasted_iota(jnp.int32, (1, span), 1)
            allowed = allowed & (key <= place)
        s = jnp.where(allowed, dot_nt(q, k), MASKED)
        old = top[qg, at]
        new = jnp.maximum(old, jnp.max(s, axis=-1, keepdims=True))
        fade = jnp.exp2((old - new) * SCALE2)
        p = jnp.exp2((s - new) * SCALE2)
        top[qg, at] = new
        total[qg, at] = fade * total[qg, at] + jnp.sum(p, axis=-1, keepdims=True)
        acc[qg, at] = fade * acc[qg, at] + dot(p.astype(jnp.bfloat16), v)

    def updates(qg, kg, diagonal):
        def chunk(c, _):
            for r in range(tok_count // tile):
                update(qg, kg, c, r, diagonal)
            return 0

        if group <= 2:
            chunk(0, 0)
        else:
            lax.fori_loop(0, group // 2, chunk, 0)

    def back(t):
        d = flipped(me, t, n)
        return remote(done.at[d], x.at[rows_of(part), my_cols], back_sem, (t,), d)

    own_back = pltpu.make_async_copy(done.at[me], x.at[rows_of(part), my_cols], own_sem.at[3])

    def finish(v):
        g = flipped(head, v, heads)
        o = (acc[g] / total[g]).astype(jnp.bfloat16)
        done[pl.ds(g * group, group)] = o.reshape(group, rows, DH)
        if v == 0:
            own_back.start()

        def give(t, _):
            back(t).start()
            return 0

        lax.fori_loop(max(v * group, 1), (v + 1) * group, give, 0)

    for u in range(heads):
        if u == 0:
            for copy in own:
                copy.wait()

        def arrive(t, _):
            for copy in copies(t):
                copy.wait_recv()
            return 0

        lax.fori_loop(max(u * group, 1), (u + 1) * group, arrive, 0)
        for g in range(1, group):
            passed(u, g).start()
        a = flipped(head, u, heads)

        def prepare(w, _):
            row = ck[a * group + w].astype(jnp.float32)
            column = jnp.transpose(jnp.broadcast_to(row, (128, tok_count)))
            done_rows = pl.ds(pl.multiple_of(w * rows, rows), rows)
            acc[a] = column
            cq[a, done_rows] = acc[a, rows_of(part)]
            return 0

        lax.fori_loop(0, group, prepare, 0)
        top[a] = jnp.full(top.shape[1:], MASKED, jnp.float32)
        total[a] = jnp.zeros(total.shape[1:], jnp.float32)
        acc[a] = jnp.zeros(acc.shape[1:], jnp.float32)
        for g in range(1, group):
            passed(u, g).wait_recv()
        updates(a, a, True)
        for v in reversed(range(u)):
            b = flipped(head, v, heads)
            updates(jnp.maximum(a, b), jnp.minimum(a, b), False)
            if u == heads - 1:
                finish(v)
    finish(heads - 1)

    @pl.when(me > 0)
    def _():
        prev_copy.wait_recv()

    window_heads(me == 0, local_ref, prev, local_out)

    @pl.when(me < n - 1)
    def _():
        prev_copy.wait_send()

    def settle(t, _):
        for copy in copies(t):
            copy.wait_send()
        back(t).wait()
        return 0

    lax.fori_loop(1, n, settle, 0)
    own_back.wait()
    for u in range(heads):
        for g in range(1, group):
            passed(u, g).wait_send()
    for copy in weights:
        copy.wait()
    project(place, across, local_out, x, wl, wr, out_ref, tiles_out, tiles_in, out_sem, in_sem)


def project(me, across, local_ref, x, wl_ref, wr_ref, out_ref, send, recv, send_sem, recv_sem):
    cols = out_ref.shape[1]
    pieces = send.shape[1]
    tile = cols // pieces
    corner = lax.rem(across[0] + 2, 4)

    def product(owner, c):
        at = pl.ds(pl.multiple_of(owner * cols + c * tile, tile), tile)
        return dot(local_ref[...], wl_ref[:, at]) + dot(x[...], wr_ref[:, at])

    def hand(kind, c, value, device):
        send[kind, c] = value.astype(jnp.bfloat16)
        return pltpu.make_async_remote_copy(
            src_ref=send.at[kind, c], dst_ref=recv.at[kind, c],
            send_sem=send_sem.at[kind, c], recv_sem=recv_sem.at[kind, c],
            device_id={"heads": device}, device_id_type=MESH)

    order = [c + half * (pieces // 2) for c in range(pieces // 2) for half in range(2)]
    way = [c // (pieces // 2) for c in range(pieces)]
    copies = {}
    for kind in range(2):
        for c in order:
            device = across[way[c]]
            copies[kind, c] = hand(kind, c, product(device if kind else corner, c), device)
            copies[kind, c].start()
    for c in order:
        device = across[1 - way[c]]
        value = product(device, c)
        copies[0, c].wait_recv()
        copies[2, c] = hand(2, c, value + recv[0, c].astype(jnp.float32), device)
        copies[2, c].start()
    for c in order:
        value = product(me, c)
        copies[1, c].wait_recv()
        value = value + recv[1, c].astype(jnp.float32)
        copies[2, c].wait_recv()
        value = value + recv[2, c].astype(jnp.float32)
        out_ref[:, c * tile:(c + 1) * tile] = value.astype(jnp.bfloat16)
    for copy in copies.values():
        copy.wait_send()


def body(local_qkv, routed_qkv, clusters, wo_local, wo_routed):
    tok_count = routed_qkv.shape[1]
    heads = clusters.shape[0]
    n = lax.axis_size("seq")
    group = n // heads
    rows = tok_count // group
    cols = wo_local.shape[1] // lax.axis_size("heads")
    slots = (3, 4, tok_count, cols // 4)
    DMA = pltpu.SemaphoreType.DMA
    return pl.pallas_call(
        functools.partial(layer_kernel, n, heads),
        out_shape=jax.ShapeDtypeStruct((tok_count, cols), jnp.bfloat16),
        in_specs=[vmem()] * 3 + [pl.BlockSpec(memory_space=pl.ANY)] * 2,
        out_specs=vmem(),
        scratch_shapes=[
            pltpu.VMEM((2,) + local_qkv.shape[1:], jnp.bfloat16),
            pltpu.VMEM((n, rows, DH), jnp.bfloat16),
            pltpu.VMEM((n, 2, tok_count, DH), jnp.bfloat16),
            pltpu.VMEM((n, 1, tok_count), jnp.int32),
            pltpu.VMEM((heads, tok_count, 128), jnp.float32),
            pltpu.VMEM((heads, tok_count, DH), jnp.float32),
            pltpu.VMEM((heads, tok_count, 1), jnp.float32),
            pltpu.VMEM((heads, tok_count, 1), jnp.float32),
            pltpu.VMEM((n, rows, DH), jnp.bfloat16),
            DMA((4,)), DMA((2, n)), DMA((2, n)), DMA((2, n)),
            DMA((2, heads, max(group - 1, 1))), DMA((2, n)), DMA((2,)),
            pltpu.VMEM(local_qkv.shape[1:], jnp.bfloat16),
            pltpu.VMEM((tok_count, heads * DH), jnp.bfloat16),
            pltpu.VMEM(wo_local.shape, jnp.bfloat16),
            pltpu.VMEM(wo_routed.shape, jnp.bfloat16),
            pltpu.VMEM(slots, jnp.bfloat16),
            pltpu.VMEM(slots, jnp.bfloat16),
            DMA(slots[:2]), DMA(slots[:2]), DMA((2,)),
        ],
        cost_estimate=pl.CostEstimate(
            flops=4 << 30, bytes_accessed=200 << 20, transcendentals=8 << 20),
        compiler_params=pltpu.CompilerParams(
            vmem_limit_bytes=VMEM_LIMIT, collective_id=0, has_side_effects=True),
    )(routed_qkv, clusters.reshape(heads, 1, tok_count), local_qkv, wo_local, wo_routed)


ROUNDS = 4
BACK = 2
CLUSTERS = 128


def chain_kernel(n, routed, ids, local, wl_any, wr_any, out_ref,
                 kaug, vaug, q_own, qbuf, qmask, id_key, id_query, opart, spart, osend, orecv, ssend, srecv, bsend, brecv, tsend, trecv,
                 lq, lkv, lout, x, wl, wr, rsend, rrecv,
                 load_sem, key_sem, kid_sem, far_sem, fid_sem, near_sem, nid_sem, q_sem, qid_sem,
                 o_sem, s_sem, b_sem, t_sem, halo_sem, w_sem, r_sem):
    tok = q_own.shape[0]
    width = q_own.shape[1]
    heads = width // DH
    rounds = q_sem.shape[3]
    rows = tok // rounds
    cols = out_ref.shape[1]
    half_cols = cols // 2
    me = lax.axis_index("seq")
    z = lax.div(me, 2)
    core = lax.rem(me, 2)
    partner = me + 1 - 2 * core
    place = lax.axis_index("heads")
    across = (place + 1 - 2 * lax.rem(place, 2), lax.rem(place + 2, 4))
    corner = lax.rem(across[0] + 2, 4)

    def start(r):
        return (rounds - 1 - r) * rows

    def at(r):
        return pl.ds(pl.multiple_of(start(r), rows), rows)

    def remote(src, dst, sem, index, **device):
        return pltpu.make_async_remote_copy(
            src_ref=src, dst_ref=dst, send_sem=sem.at[(0,) + index], recv_sem=sem.at[(1,) + index],
            device_id=device, device_id_type=MESH)

    def guarded(cond, f, *args):
        @pl.when(cond)
        def _():
            f(*args)

    barrier = pltpu.get_barrier_semaphore()
    greeted = jnp.int32(len(across))
    for d in (-4, -2, -1, 1, 2, 4):
        there = (me + d >= 0) & (me + d < n)

        @pl.when(there)
        def _():
            pl.semaphore_signal(barrier, inc=1, device_id={"seq": me + d}, device_id_type=MESH)

        greeted = greeted + there.astype(jnp.int32)
    for device in across:
        pl.semaphore_signal(barrier, inc=1, device_id={"heads": device}, device_id_type=MESH)

    mine = pl.ds(pl.multiple_of(core * tok, tok), tok)
    loads = []
    for i, aug in enumerate((kaug, vaug)):
        for h in range(heads):
            loads.append((routed.at[1 + i, :, h * DH:(h + 1) * DH], aug.at[0, h, mine, pl.ds(0, DH)]))
    loads.append((routed.at[0], q_own))
    loads.append((ids, id_key.at[0, core]))
    loads.append((local.at[0], lq))
    loads.append((local.at[pl.ds(1, 2)], lkv.at[:, pl.ds(tok, tok)]))
    loads = [pltpu.make_async_copy(a, b, load_sem.at[i]) for i, (a, b) in enumerate(loads)]
    for copy in loads:
        copy.start()

    def share(aug, i, h, part, src, sem, device):
        return remote(src, aug.at[part, h, mine, pl.ds(0, DH)], sem, (i, h), seq=device)

    both = ((0, kaug), (1, vaug))
    given = [(i, aug, h, routed.at[1 + i, :, h * DH:(h + 1) * DH]) for h in range(heads) for i, aug in both]
    keys = [share(aug, i, h, 0, src, key_sem, partner) for i, aug, h, src in given]
    keys.append(remote(ids, id_key.at[0, core], kid_sem, (), seq=partner))
    far = [share(aug, i, h, 1, src, far_sem, me + 2) for i, aug, h, src in given if h >= BACK]
    far_id = remote(ids, id_key.at[1, core], fid_sem, (), seq=me + 2)
    near = [share(aug, i, h, 1, aug.at[1, h, mine, pl.ds(0, DH)], near_sem, partner)
            for i, aug, h, src in given if h >= BACK]
    near_id = remote(id_key.at[1, core], id_key.at[1, core], nid_sem, (), seq=partner)

    def halo(r):
        return remote(local.at[pl.ds(1, 2), at(r)], lkv.at[:, at(r)], halo_sem, (r,), seq=me + 1)

    weights = (
        pltpu.make_async_copy(wl_any, wl, w_sem.at[0]),
        pltpu.make_async_copy(wr_any, wr, w_sem.at[1]),
    )

    def q_copy(to, slot, r):
        here = qbuf.at[slot, at(r)]
        if to == 0:
            first = pl.ds(0, BACK * DH)
            here = qbuf.at[slot, at(r), first]
            src = routed.at[0, at(r), first] if slot == 0 else here
        else:
            src = routed.at[0, at(r)]
        return remote(src, here, q_sem, (to, slot, r), seq=2 * to + core)

    def qid_copy(to, slot):
        here = id_query.at[slot]
        return remote(here if to == 0 and slot > 0 else ids, here, qid_sem, (to, slot), seq=2 * to + core)

    def b_copies(r):
        return (remote(bsend.at[r], brecv.at[r], b_sem, (r,), seq=me + 2),
                remote(tsend.at[r], trecv.at[r], t_sem, (r,), seq=me + 2))

    sent = ((1, 1, 2), (1, 2, 3), (2, 2, 3))

    def o_copies(source, slot, r):
        def one(src, dst, sem):
            return pltpu.make_async_remote_copy(
                src_ref=src.at[slot, r], dst_ref=dst.at[source, r],
                send_sem=sem.at[0, slot, r], recv_sem=sem.at[1, source, r],
                device_id={"seq": 2 * (slot + 2) + core}, device_id_type=MESH)

        return one(osend, orecv, o_sem), one(ssend, srecv, s_sem)

    def r_copy(kind, r, half):
        device = across[half] if kind < 2 else across[1 - half]
        return remote(rsend.at[kind, r, half], rrecv.at[kind, r, half], r_sem, (kind, r, half), heads=device)

    pl.semaphore_wait(barrier, greeted)

    @pl.when(z == 0)
    def _():
        far_id.start()
        for copy in far:
            copy.start()

    @pl.when(z == 1)
    def _():
        qid_copy(0, 0).start()

    for to, slot, chip in sent:
        guarded(z == chip, qid_copy(to, slot).start)

    for copy in keys:
        copy.start()

    def ask(r, _):
        for to, slot, chip in sent + ((0, 0, 1),):
            guarded(z == chip, q_copy(to, slot, r).start)

        guarded((me < n - 1) & (me != 1), halo(r).start)
        return 0

    lax.fori_loop(0, rounds, ask, 0)
    for copy in weights:
        copy.start()

    def table(row, on, off):
        c = lax.broadcasted_iota(jnp.int32, (CLUSTERS, tok), 0)
        t = jnp.where(c == row, jnp.float32(on), jnp.float32(off))
        return jnp.transpose(t).astype(jnp.bfloat16)

    def mask_of(slot, id_ref, count=heads):
        for h in range(count):
            qmask[slot, h] = table(id_ref[h:h + 1, :], 0.0, MASKED)

    def key_table(part, c, first=0):
        where = pl.ds(pl.multiple_of(c * tok, tok), tok)
        for h in range(first, heads):
            kaug[part, h, where, DH:] = table(id_key[part, c, h:h + 1, :], 1.0, 0.0)

    for h in range(heads):
        vaug[0, h, :, DH:] = jnp.ones((2 * tok, DH), jnp.bfloat16)

    @pl.when(me == 0)
    def _():
        lkv[:, :tok] = jnp.zeros((2, tok, width), jnp.bfloat16)

    mask_of(0, ids)
    for copy in loads:
        copy.wait()
    key_table(0, core)
    for copy in keys:
        copy.wait_recv()
    key_table(0, 1 - core)

    lane = lax.broadcasted_iota(jnp.int32, (1, DH), 1)

    def softmax(part, h, q, masks, count=None, allowed=None):
        s = dot_nt(jnp.concatenate([q, masks], axis=1), kaug[part, h, :count])
        if allowed is not None:
            own = jnp.where(allowed, s[:rows], MASKED)
            s = own if s.shape[0] == rows else jnp.concatenate([own, s[rows:]], axis=0)
        top = jnp.max(s, axis=-1, keepdims=True)
        p = jnp.exp2((s - top) * SCALE2).astype(jnp.bfloat16)
        o = dot(p, vaug[part, h, :count])
        total = o[:, DH:]
        return o[:, :DH] / total, top * SCALE2 + jnp.log2(total)

    def attend_own(r):
        i = core * tok + start(r) + lax.broadcasted_iota(jnp.int32, (rows, 1), 0)
        for c in range(2):
            @pl.when(core == c)
            def _():
                count = (c + 1) * tok
                allowed = lax.broadcasted_iota(jnp.int32, (1, count), 1) <= i
                stat = jnp.zeros((rows, DH), jnp.float32)
                for h in range(heads):
                    hc = slice(h * DH, (h + 1) * DH)
                    o, level = softmax(0, h, q_own[at(r), hc], qmask[0, h, at(r)], count, allowed)
                    opart[0, at(r), hc] = o
                    stat = jnp.where(lane == h, level, stat)
                spart[0, at(r)] = stat

    def attend(first, r):
        count = 4 - first
        i = core * tok + start(r) + lax.broadcasted_iota(jnp.int32, (rows, 1), 0)
        allowed = lax.broadcasted_iota(jnp.int32, (1, 2 * tok), 1) <= i
        stat = jnp.zeros((rows, DH), jnp.float32)
        stats = jnp.zeros((count * rows, DH), jnp.float32)
        for h in range(heads):
            hc = slice(h * DH, (h + 1) * DH)
            q, masks = q_own[at(r), hc], qmask[0, h, at(r)]
            others = first > 1 or h < BACK
            if others:
                q = jnp.concatenate([q, qbuf[first - 1:, at(r), hc].reshape(count * rows, DH)], axis=0)
                masks = jnp.concatenate([masks, qmask[first:, h, at(r)].reshape(count * rows, DH)], axis=0)
            o, level = softmax(0, h, q, masks, None, allowed)
            if first == 1:
                x[at(r), hc] = o[:rows].astype(jnp.bfloat16)
            else:
                opart[0, at(r), hc] = o[:rows]
                stat = jnp.where(lane == h, level[:rows], stat)
            if others:
                o = o[rows:]
                if first == 1:
                    bsend[r, :, :, hc] = o.astype(jnp.bfloat16).reshape(count, rows, DH)
                elif first == 3:
                    osend[1, r, :, hc] = o.astype(jnp.bfloat16)
                else:
                    opart[1:, at(r), hc] = o.reshape(count, rows, DH)
                stats = jnp.where(lane == h, level[rows:], stats)
            if h == BACK - 1 and first == 1:
                for i in range(count):
                    tsend[r, i] = stat_rows(stats[i * rows:(i + 1) * rows])
                for copy in b_copies(r):
                    copy.start()
        if first > 1:
            spart[0, at(r)] = stat
        if first == 3:
            ssend[1, r] = stat_rows(stats)
            for copy in o_copies(1, 1, r):
                copy.start()
        elif first == 2:
            spart[1:, at(r)] = stats.reshape(count, rows, DH)

    def attend_far(r):
        stat = jnp.zeros((3 * rows, DH), jnp.float32)
        before = spart[:, at(r)].reshape(3 * rows, DH)
        levels_back = jnp.concatenate([stat_columns(trecv[r, i]) for i in range(3)], axis=0)
        for h in range(heads):
            hc = slice(h * DH, (h + 1) * DH)
            if h < BACK:
                o = brecv[r, :, :, hc].reshape(3 * rows, DH).astype(jnp.float32)
                level = levels_back[:, h:h + 1]
            else:
                q = jnp.concatenate([q_own[at(r), hc], qbuf[1:, at(r), hc].reshape(2 * rows, DH)], axis=0)
                masks = jnp.concatenate([qmask[0, h, at(r)], qmask[2:, h, at(r)].reshape(2 * rows, DH)], axis=0)
                o, level = softmax(1, h, q, masks)
            level_near = before[:, h:h + 1]
            high = jnp.maximum(level, level_near)
            w = jnp.exp2(level - high)
            w_near = jnp.exp2(level_near - high)
            total = w + w_near
            o = ((w * o + w_near * opart[:, at(r), hc].reshape(3 * rows, DH)) / total).astype(jnp.bfloat16)
            x[at(r), hc] = o[:rows]
            for slot in range(2):
                osend[slot, r, :, hc] = o[(slot + 1) * rows:(slot + 2) * rows]
            stat = jnp.where(lane == h, high + jnp.log2(total), stat)
        for slot in (1, 0):
            ssend[slot, r] = stat_rows(stat[(slot + 1) * rows:(slot + 2) * rows])
            for copy in o_copies(0, slot, r):
                copy.start()

    def stat_columns(packed):
        return jnp.transpose(jnp.concatenate([packed, jnp.zeros((DH - 8, DH), jnp.float32)], axis=0))[:rows]

    def stat_rows(stat):
        return jnp.transpose(jnp.concatenate([stat] * (DH // rows), axis=0))[:8]

    def window(r):
        i = lax.broadcasted_iota(jnp.int32, (rows, rows + WINDOW), 0)
        c = lax.broadcasted_iota(jnp.int32, (rows, rows + WINDOW), 1)
        lowest = jnp.where(me == 0, WINDOW - start(r), 0)
        allowed = (c > i) & (c <= i + WINDOW) & (c >= lowest)
        span = pl.ds(pl.multiple_of(start(r), rows), rows + WINDOW)
        guarded(me > 0, halo(r).wait_recv)

        def head(h, _):
            hc = pl.ds(pl.multiple_of(h * DH, DH), DH)
            s = jnp.where(allowed, dot_nt(lq[at(r), hc], lkv[0, span, hc]), MASKED)
            top = jnp.max(s, axis=-1, keepdims=True)
            p = jnp.exp2((s - top) * SCALE2)
            total = jnp.sum(p, axis=-1, keepdims=True)
            o = dot(p.astype(jnp.bfloat16), lkv[1, span, hc]) / total
            lout[at(r), hc] = o.astype(jnp.bfloat16)
            return 0

        lax.fori_loop(0, heads, head, 0, unroll=True)

    def merge(sources, r):
        levels = [spart[0, at(r)]]
        for source in sources:
            for copy in o_copies(source, 0, r):
                copy.wait_recv()
            levels.append(stat_columns(srecv[source, r]))
        high = functools.reduce(jnp.maximum, levels)
        ws = [jnp.exp2(level - high) for level in levels]
        total = sum(ws[1:], ws[0])
        ws = [w / total for w in ws]
        for h in range(heads):
            hc = slice(h * DH, (h + 1) * DH)
            o = ws[0][:, h:h + 1] * opart[0, at(r), hc]
            for source, w in zip(sources, ws[1:]):
                o = o + w[:, h:h + 1] * orecv[source, r, :, hc].astype(jnp.float32)
            x[at(r), hc] = o.astype(jnp.bfloat16)

    def product(owner, half, r):
        c = pl.ds(pl.multiple_of(owner * cols + half * half_cols, half_cols), half_cols)
        return dot(lout[at(r)], wl[:, c]) + dot(x[at(r)], wr[:, c])

    def hand(kind, r, half, value):
        rsend[kind, r, half] = value.astype(jnp.bfloat16)
        r_copy(kind, r, half).start()

    def reduce1(r):
        for half in range(2):
            hand(0, r, half, product(corner, half, r))
        for half in range(2):
            hand(1, r, half, product(across[half], half, r))

    def reduce2(r):
        for half in range(2):
            value = product(across[1 - half], half, r)
            r_copy(0, r, half).wait_recv()
            hand(2, r, half, value + rrecv[0, r, half].astype(jnp.float32))

    def reduce3(r):
        for half in range(2):
            value = product(place, half, r)
            for kind in (1, 2):
                r_copy(kind, r, half).wait_recv()
                value = value + rrecv[kind, r, half].astype(jnp.float32)
            out_ref[at(r), half * half_cols:(half + 1) * half_cols] = value.astype(jnp.bfloat16)

    def reduce(t):
        for late, stage in ((0, reduce1), (1, reduce2), (2, reduce3)):
            guarded((t >= late) & (t < rounds + late), stage, t - late)

    def both_weights():
        for copy in weights:
            copy.wait()

    @pl.when(z == 0)
    def _():
        def step(t, _):
            @pl.when(t < rounds)
            def _():
                @pl.when(t == 0)
                def _():
                    for slot in range(3):
                        qid_copy(0, slot).wait_recv()
                        mask_of(1 + slot, id_query.at[slot], BACK)

                for slot in range(3):
                    q_copy(0, slot, t).wait_recv()
                attend(1, t)
                guarded(me == 1, halo(t).start)
                window(t)
                guarded(t == 0, both_weights)

            reduce(t)
            return 0

        lax.fori_loop(0, rounds + 2, step, 0)
        far_id.wait_send()
        for copy in far:
            copy.wait_send()

    @pl.when(z == 1)
    def _():
        for slot in (1, 2):
            qid_copy(1, slot).wait_recv()
            qid_copy(0, slot).start()
            mask_of(1 + slot, id_query.at[slot])
        vaug[1, BACK:, :, DH:] = vaug[0, BACK:, :, DH:]

        def first(t, _):
            for slot in (1, 2):
                q_copy(1, slot, t).wait_recv()
                q_copy(0, slot, t).start()
            attend(2, t)
            return 0

        lax.fori_loop(0, rounds, first, 0)
        far_id.wait_recv()
        near_id.start()
        key_table(1, core, BACK)
        for here, there in zip(far, near):
            here.wait_recv()
            there.start()
        near_id.wait_recv()
        key_table(1, 1 - core, BACK)
        for copy in near:
            copy.wait_recv()
        both_weights()

        def second(t, _):
            @pl.when(t < rounds)
            def _():
                for copy in b_copies(t):
                    copy.wait_recv()
                attend_far(t)
                window(t)

            reduce(t)
            return 0

        lax.fori_loop(0, rounds + 2, second, 0)
        near_id.wait_send()
        for copy in near:
            copy.wait_send()

    @pl.when(z >= 2)
    def _():
        @pl.when(z == 2)
        def _():
            qid_copy(2, 2).wait_recv()
            mask_of(3, id_query.at[2])

        def first(t, _):
            @pl.when(z == 2)
            def _():
                q_copy(2, 2, t).wait_recv()
                attend(3, t)

            guarded(z == 3, attend_own, t)
            return 0

        lax.fori_loop(0, rounds, first, 0)

        def second(t, _):
            window(t)
            return 0

        lax.fori_loop(0, rounds, second, 0)
        both_weights()

        def third(t, _):
            @pl.when(t < rounds)
            def _():
                guarded(z == 2, merge, (0,), t)
                guarded(z == 3, merge, (0, 1), t)

            reduce(t)
            return 0

        lax.fori_loop(0, rounds + 2, third, 0)

    for copy in keys:
        copy.wait_send()

    sent = sent + ((0, 0, 1), (0, 1, 1), (0, 2, 1))
    for to, slot, chip in sent:
        guarded(z == chip, qid_copy(to, slot).wait_send)

    def settle(r, _):
        for to, slot, chip in sent:
            guarded(z == chip, q_copy(to, slot, r).wait_send)
        guarded(me < n - 1, halo(r).wait_send)

        @pl.when(z == 0)
        def _():
            for copy in b_copies(r):
                copy.wait_send()

        for slot in range(2):
            @pl.when((z == 1) | ((z == 2) & (slot == 1)))
            def _():
                for copy in o_copies(0, slot, r):
                    copy.wait_send()

        return 0

    lax.fori_loop(0, rounds, settle, 0)

    def settle_sums(r, _):
        for kind in range(3):
            for half in range(2):
                r_copy(kind, r, half).wait_send()
        return 0

    lax.fori_loop(0, rounds, settle_sums, 0)


def chain_body(local_qkv, routed_qkv, clusters, wo_local, wo_routed):
    tok, width = routed_qkv.shape[1:]
    heads = clusters.shape[0]
    n = lax.axis_size("seq")
    rows = tok // ROUNDS
    cols = wo_local.shape[1] // lax.axis_size("heads")
    DMA = pltpu.SemaphoreType.DMA
    any_spec = pl.BlockSpec(memory_space=pl.ANY)

    def bf16(*shape):
        return pltpu.VMEM(shape, jnp.bfloat16)

    def f32(*shape):
        return pltpu.VMEM(shape, jnp.float32)

    slots = (3, ROUNDS, 2, rows, cols // 2)
    return pl.pallas_call(
        functools.partial(chain_kernel, n),
        out_shape=jax.ShapeDtypeStruct((tok, cols), jnp.bfloat16),
        in_specs=[any_spec, vmem(), any_spec, any_spec, any_spec],
        out_specs=vmem(),
        scratch_shapes=[
            bf16(2, heads, 2 * tok, 2 * DH), bf16(2, heads, 2 * tok, 2 * DH),
            bf16(tok, width), bf16(3, tok, width), bf16(4, heads, tok, CLUSTERS),
            pltpu.VMEM((2, 2, heads, tok), jnp.int32), pltpu.VMEM((3, heads, tok), jnp.int32),
            f32(3, tok, width), f32(3, tok, DH),
            bf16(2, ROUNDS, rows, width), bf16(2, ROUNDS, rows, width),
            f32(2, ROUNDS, 8, DH), f32(2, ROUNDS, 8, DH),
            bf16(ROUNDS, 3, rows, BACK * DH), bf16(ROUNDS, 3, rows, BACK * DH),
            f32(ROUNDS, 3, 8, DH), f32(ROUNDS, 3, 8, DH),
            bf16(tok, width), bf16(2, 2 * tok, width), bf16(tok, width), bf16(tok, width),
            bf16(*wo_local.shape), bf16(*wo_routed.shape), bf16(*slots), bf16(*slots),
            DMA((2 * heads + 4,)), DMA((2, 2, heads)), DMA((2,)), DMA((2, 2, heads)), DMA((2,)),
            DMA((2, 2, heads)), DMA((2,)), DMA((2, 3, 3, ROUNDS)), DMA((2, 3, 3)),
            DMA((2, 2, ROUNDS)), DMA((2, 2, ROUNDS)), DMA((2, ROUNDS)), DMA((2, ROUNDS)),
            DMA((2, ROUNDS)), DMA((2,)), DMA((2,) + slots[:3]),
        ],
        cost_estimate=pl.CostEstimate(
            flops=8 << 30, bytes_accessed=20 << 20, transcendentals=8 << 20),
        compiler_params=pltpu.CompilerParams(
            vmem_limit_bytes=VMEM_LIMIT, collective_id=1, has_side_effects=True),
    )(routed_qkv, clusters, local_qkv, wo_local, wo_routed)


def solution(mesh):
    return jax.shard_map(
        chain_body if mesh.shape["seq"] == 8 else body,
        mesh=mesh,
        in_specs=(
            P(None, "seq", "heads"),
            P(None, "seq", "heads"),
            P("heads", "seq"),
            P("heads", None),
            P("heads", None),
        ),
        out_specs=P("seq", "heads"),
        check_vma=False,
    )
```

```python
import functools
import math

import jax
import jax.numpy as jnp
from jax import lax
from jax.experimental import pallas as pl
from jax.experimental.pallas import tpu as pltpu
from jax.sharding import PartitionSpec as P

DH = 128
WINDOW = 512
MASKED = -1e30
SCALE2 = math.log2(math.e) / math.sqrt(DH)
VMEM_LIMIT = 56 << 20

NT = (((1,), (1,)), ((), ()))
MESH = pl.DeviceIdType.MESH


def vmem():
    return pl.BlockSpec(memory_space=pltpu.VMEM)


def dot_nt(a, b):
    return lax.dot_general(a, b, NT, preferred_element_type=jnp.float32)


def dot(a, b):
    return jnp.dot(a, b, preferred_element_type=jnp.float32)


def window_heads(is_first, own_ref, prev_ref, out_ref):
    tok_count, width = out_ref.shape
    rows = min(256, tok_count)
    span = rows + WINDOW
    for i in range(tok_count // rows):
        r = lax.broadcasted_iota(jnp.int32, (rows, span), 0)
        c = lax.broadcasted_iota(jnp.int32, (rows, span), 1)
        from_prev = WINDOW - i * rows
        lowest = jnp.where(is_first, from_prev, 0)
        allowed = (c > r) & (c <= r + WINDOW) & (c >= lowest)
        for h in range(width // DH):
            cols = slice(h * DH, (h + 1) * DH)
            q = own_ref[0, i * rows:(i + 1) * rows, cols]
            k = jnp.concatenate(
                [prev_ref[0, i * rows:, cols], own_ref[1, :(i + 1) * rows, cols]], axis=0)
            v = jnp.concatenate(
                [prev_ref[1, i * rows:, cols], own_ref[2, :(i + 1) * rows, cols]], axis=0)
            s = jnp.where(allowed, dot_nt(q, k), MASKED)
            top = jnp.max(s, axis=-1, keepdims=True)
            p = jnp.exp2((s - top) * SCALE2)
            total = jnp.sum(p, axis=-1, keepdims=True)
            o = dot(p.astype(jnp.bfloat16), v) / total
            out_ref[i * rows:(i + 1) * rows, cols] = o.astype(jnp.bfloat16)


def flipped(me, t, n):
    out = 0
    bit = 1
    while bit < n:
        out = out + lax.rem(lax.div(me, bit) + lax.div(jnp.int32(t), bit), 2) * bit
        bit *= 2
    return out


def layer_kernel(n, heads, qkv_ref, id_ref, local_ref, wl_any, wr_any, out_ref, prev, rq, kv, ck, cq, acc, top, total, done,
                   own_sem, q_sem, kv_sem, id_sem, pass_sem, back_sem, prev_sem,
                 local_out, x, wl, wr, tiles_out, tiles_in, out_sem, in_sem, w_sem):
    group = n // heads
    tok_count = x.shape[0]
    rows = tok_count // group
    tile = min(256, tok_count)
    me = lax.axis_index("seq")
    head = lax.div(me, group)
    part = lax.rem(me, group)

    def rows_of(p):
        return pl.ds(pl.multiple_of(p * rows, rows), rows)

    def remote(src, dst, sem, index, device):
        return pltpu.make_async_remote_copy(
            src_ref=src, dst_ref=dst, send_sem=sem.at[(0,) + index], recv_sem=sem.at[(1,) + index],
            device_id={"seq": device}, device_id_type=MESH)

    def copies(t):
        d = flipped(me, t, n)
        h = pl.ds(pl.multiple_of(lax.div(d, group) * DH, DH), DH)
        p = rows_of(lax.rem(d, group))
        return (
            remote(id_ref.at[lax.div(d, group)], ck.at[me], id_sem, (t,), d),
            remote(qkv_ref.at[pl.ds(1, 2), p, h], kv.at[me, :, p], kv_sem, (t,), d),
            remote(qkv_ref.at[0, p, h], rq.at[me], q_sem, (t,), d),
        )

    def passed(u, g):
        src = kv.at[pl.ds(flipped(head, u, heads) * group, group), :, rows_of(part)]
        return remote(src, src, pass_sem, (u, g - 1), flipped(me, g, n))

    barrier = pltpu.get_barrier_semaphore()

    def greet(t, _):
        pl.semaphore_signal(barrier, inc=1, device_id={"seq": flipped(me, t, n)},
                            device_id_type=MESH)
        return 0

    lax.fori_loop(1, n, greet, 0)
    place = lax.axis_index("heads")
    across = (place + 1 - 2 * lax.rem(place, 2), lax.rem(place + 2, 4))
    for device in across:
        pl.semaphore_signal(barrier, inc=1, device_id={"heads": device}, device_id_type=MESH)
    weights = (
        pltpu.make_async_copy(wl_any, wl, w_sem.at[0]),
        pltpu.make_async_copy(wr_any, wr, w_sem.at[1]),
    )
    my_cols = pl.ds(pl.multiple_of(head * DH, DH), DH)
    own = (
        pltpu.make_async_copy(id_ref.at[head], ck.at[me], own_sem.at[0]),
        pltpu.make_async_copy(qkv_ref.at[pl.ds(1, 2), rows_of(part), my_cols],
                              kv.at[me, :, rows_of(part)], own_sem.at[1]),
        pltpu.make_async_copy(qkv_ref.at[0, rows_of(part), my_cols], rq.at[me], own_sem.at[2]),
    )
    for copy in own:
        copy.start()
    pl.semaphore_wait(barrier, n - 1 + len(across))

    def send(t, _):
        for copy in copies(t):
            copy.start()
        return 0

    lax.fori_loop(1, n, send, 0)
    for copy in weights:
        copy.start()
    prev_copy = remote(local_ref.at[pl.ds(1, 2)], prev, prev_sem, (), lax.rem(me + 1, n))

    @pl.when(me < n - 1)
    def _():
        prev_copy.start()

    @pl.when(me == 0)
    def _():
        prev[...] = jnp.zeros_like(prev)

    def update(qg, kg, c, r, diagonal):
        blocks = min(2, group)
        if diagonal and group == 2 and rows == tile:
            blocks = r + 1
        span = blocks * tok_count
        at = slice(r * tile, (r + 1) * tile)
        first = kg * group + c * 2
        per = tile // rows
        q = rq[pl.ds(qg * group + r * per, per)].reshape(tile, DH)
        k = kv[pl.ds(first, blocks), 0].reshape(span, DH)
        v = kv[pl.ds(first, blocks), 1].reshape(span, DH)
        ids = jnp.concatenate([ck[first + i] for i in range(blocks)], axis=1)
        allowed = cq[qg, at, :1] == ids.astype(jnp.float32)
        if diagonal:
            i = r * tile + lax.broadcasted_iota(jnp.int32, (tile, 1), 0)
            shift = rows.bit_length() - 1
            place = (i >> shift) * tok_count + part * rows + (i & (rows - 1))
            key = c * 2 * tok_count + lax.broadcasted_iota(jnp.int32, (1, span), 1)
            allowed = allowed & (key <= place)
        s = jnp.where(allowed, dot_nt(q, k), MASKED)
        old = top[qg, at]
        new = jnp.maximum(old, jnp.max(s, axis=-1, keepdims=True))
        fade = jnp.exp2((old - new) * SCALE2)
        p = jnp.exp2((s - new) * SCALE2)
        top[qg, at] = new
        total[qg, at] = fade * total[qg, at] + jnp.sum(p, axis=-1, keepdims=True)
        acc[qg, at] = fade * acc[qg, at] + dot(p.astype(jnp.bfloat16), v)

    def updates(qg, kg, diagonal):
        def chunk(c, _):
            for r in range(tok_count // tile):
                update(qg, kg, c, r, diagonal)
            return 0

        if group <= 2:
            chunk(0, 0)
        else:
            lax.fori_loop(0, group // 2, chunk, 0)

    def back(t):
        d = flipped(me, t, n)
        return remote(done.at[d], x.at[rows_of(part), my_cols], back_sem, (t,), d)

    own_back = pltpu.make_async_copy(done.at[me], x.at[rows_of(part), my_cols], own_sem.at[3])

    def finish(v):
        g = flipped(head, v, heads)
        o = (acc[g] / total[g]).astype(jnp.bfloat16)
        done[pl.ds(g * group, group)] = o.reshape(group, rows, DH)
        if v == 0:
            own_back.start()

        def give(t, _):
            back(t).start()
            return 0

        lax.fori_loop(max(v * group, 1), (v + 1) * group, give, 0)

    for u in range(heads):
        if u == 0:
            for copy in own:
                copy.wait()

        def arrive(t, _):
            for copy in copies(t):
                copy.wait_recv()
            return 0

        lax.fori_loop(max(u * group, 1), (u + 1) * group, arrive, 0)
        for g in range(1, group):
            passed(u, g).start()
        a = flipped(head, u, heads)

        def prepare(w, _):
            row = ck[a * group + w].astype(jnp.float32)
            column = jnp.transpose(jnp.broadcast_to(row, (128, tok_count)))
            done_rows = pl.ds(pl.multiple_of(w * rows, rows), rows)
            acc[a] = column
            cq[a, done_rows] = acc[a, rows_of(part)]
            return 0

        lax.fori_loop(0, group, prepare, 0)
        top[a] = jnp.full(top.shape[1:], MASKED, jnp.float32)
        total[a] = jnp.zeros(total.shape[1:], jnp.float32)
        acc[a] = jnp.zeros(acc.shape[1:], jnp.float32)
        for g in range(1, group):
            passed(u, g).wait_recv()
        updates(a, a, True)
        for v in reversed(range(u)):
            b = flipped(head, v, heads)
            updates(jnp.maximum(a, b), jnp.minimum(a, b), False)
            if u == heads - 1:
                finish(v)
    finish(heads - 1)

    @pl.when(me > 0)
    def _():
        prev_copy.wait_recv()

    window_heads(me == 0, local_ref, prev, local_out)

    @pl.when(me < n - 1)
    def _():
        prev_copy.wait_send()

    def settle(t, _):
        for copy in copies(t):
            copy.wait_send()
        back(t).wait()
        return 0

    lax.fori_loop(1, n, settle, 0)
    own_back.wait()
    for u in range(heads):
        for g in range(1, group):
            passed(u, g).wait_send()
    for copy in weights:
        copy.wait()
    project(place, across, local_out, x, wl, wr, out_ref, tiles_out, tiles_in, out_sem, in_sem)


def project(me, across, local_ref, x, wl_ref, wr_ref, out_ref, send, recv, send_sem, recv_sem):
    cols = out_ref.shape[1]
    pieces = send.shape[1]
    tile = cols // pieces
    corner = lax.rem(across[0] + 2, 4)

    def product(owner, c):
        at = pl.ds(pl.multiple_of(owner * cols + c * tile, tile), tile)
        return dot(local_ref[...], wl_ref[:, at]) + dot(x[...], wr_ref[:, at])

    def hand(kind, c, value, device):
        send[kind, c] = value.astype(jnp.bfloat16)
        return pltpu.make_async_remote_copy(
            src_ref=send.at[kind, c], dst_ref=recv.at[kind, c],
            send_sem=send_sem.at[kind, c], recv_sem=recv_sem.at[kind, c],
            device_id={"heads": device}, device_id_type=MESH)

    order = [c + half * (pieces // 2) for c in range(pieces // 2) for half in range(2)]
    way = [c // (pieces // 2) for c in range(pieces)]
    copies = {}
    for kind in range(2):
        for c in order:
            device = across[way[c]]
            copies[kind, c] = hand(kind, c, product(device if kind else corner, c), device)
            copies[kind, c].start()
    for c in order:
        device = across[1 - way[c]]
        value = product(device, c)
        copies[0, c].wait_recv()
        copies[2, c] = hand(2, c, value + recv[0, c].astype(jnp.float32), device)
        copies[2, c].start()
    for c in order:
        value = product(me, c)
        copies[1, c].wait_recv()
        value = value + recv[1, c].astype(jnp.float32)
        copies[2, c].wait_recv()
        value = value + recv[2, c].astype(jnp.float32)
        out_ref[:, c * tile:(c + 1) * tile] = value.astype(jnp.bfloat16)
    for copy in copies.values():
        copy.wait_send()


def body(local_qkv, routed_qkv, clusters, wo_local, wo_routed):
    tok_count = routed_qkv.shape[1]
    heads = clusters.shape[0]
    n = lax.axis_size("seq")
    group = n // heads
    rows = tok_count // group
    cols = wo_local.shape[1] // lax.axis_size("heads")
    slots = (3, 4, tok_count, cols // 4)
    DMA = pltpu.SemaphoreType.DMA
    return pl.pallas_call(
        functools.partial(layer_kernel, n, heads),
        out_shape=jax.ShapeDtypeStruct((tok_count, cols), jnp.bfloat16),
        in_specs=[vmem()] * 3 + [pl.BlockSpec(memory_space=pl.ANY)] * 2,
        out_specs=vmem(),
        scratch_shapes=[
            pltpu.VMEM((2,) + local_qkv.shape[1:], jnp.bfloat16),
            pltpu.VMEM((n, rows, DH), jnp.bfloat16),
            pltpu.VMEM((n, 2, tok_count, DH), jnp.bfloat16),
            pltpu.VMEM((n, 1, tok_count), jnp.int32),
            pltpu.VMEM((heads, tok_count, 128), jnp.float32),
            pltpu.VMEM((heads, tok_count, DH), jnp.float32),
            pltpu.VMEM((heads, tok_count, 1), jnp.float32),
            pltpu.VMEM((heads, tok_count, 1), jnp.float32),
            pltpu.VMEM((n, rows, DH), jnp.bfloat16),
            DMA((4,)), DMA((2, n)), DMA((2, n)), DMA((2, n)),
            DMA((2, heads, max(group - 1, 1))), DMA((2, n)), DMA((2,)),
            pltpu.VMEM(local_qkv.shape[1:], jnp.bfloat16),
            pltpu.VMEM((tok_count, heads * DH), jnp.bfloat16),
            pltpu.VMEM(wo_local.shape, jnp.bfloat16),
            pltpu.VMEM(wo_routed.shape, jnp.bfloat16),
            pltpu.VMEM(slots, jnp.bfloat16),
            pltpu.VMEM(slots, jnp.bfloat16),
            DMA(slots[:2]), DMA(slots[:2]), DMA((2,)),
        ],
        cost_estimate=pl.CostEstimate(
            flops=4 << 30, bytes_accessed=200 << 20, transcendentals=8 << 20),
        compiler_params=pltpu.CompilerParams(
            vmem_limit_bytes=VMEM_LIMIT, collective_id=0, has_side_effects=True),
    )(routed_qkv, clusters.reshape(heads, 1, tok_count), local_qkv, wo_local, wo_routed)


ROUNDS = 4
BACK = 2
CLUSTERS = 128


def chain_kernel(n, routed, ids, local, wl_any, wr_any, out_ref,
                 kaug, vaug, q_own, qbuf, qmask, id_key, id_query, opart, spart, osend, orecv, ssend, srecv, bsend, brecv, tsend, trecv,
                 lq, lkv, lout, x, wl, wr, rsend, rrecv,
                 load_sem, key_sem, kid_sem, far_sem, fid_sem, near_sem, nid_sem, q_sem, qid_sem,
                 o_sem, s_sem, b_sem, t_sem, halo_sem, w_sem, r_sem):
    tok = q_own.shape[0]
    width = q_own.shape[1]
    heads = width // DH
    rounds = q_sem.shape[3]
    rows = tok // rounds
    cols = out_ref.shape[1]
    half_cols = cols // 2
    me = lax.axis_index("seq")
    z = lax.div(me, 2)
    core = lax.rem(me, 2)
    partner = me + 1 - 2 * core
    place = lax.axis_index("heads")
    across = (place + 1 - 2 * lax.rem(place, 2), lax.rem(place + 2, 4))
    corner = lax.rem(across[0] + 2, 4)

    def start(r):
        return (rounds - 1 - r) * rows

    def at(r):
        return pl.ds(pl.multiple_of(start(r), rows), rows)

    def remote(src, dst, sem, index, **device):
        return pltpu.make_async_remote_copy(
            src_ref=src, dst_ref=dst, send_sem=sem.at[(0,) + index], recv_sem=sem.at[(1,) + index],
            device_id=device, device_id_type=MESH)

    def guarded(cond, f, *args):
        @pl.when(cond)
        def _():
            f(*args)

    barrier = pltpu.get_barrier_semaphore()
    greeted = jnp.int32(len(across))
    for d in (-4, -2, -1, 1, 2, 4):
        there = (me + d >= 0) & (me + d < n)

        @pl.when(there)
        def _():
            pl.semaphore_signal(barrier, inc=1, device_id={"seq": me + d}, device_id_type=MESH)

        greeted = greeted + there.astype(jnp.int32)
    for device in across:
        pl.semaphore_signal(barrier, inc=1, device_id={"heads": device}, device_id_type=MESH)

    mine = pl.ds(pl.multiple_of(core * tok, tok), tok)
    loads = []
    for i, aug in enumerate((kaug, vaug)):
        for h in range(heads):
            loads.append((routed.at[1 + i, :, h * DH:(h + 1) * DH], aug.at[0, h, mine, pl.ds(0, DH)]))
    loads.append((routed.at[0], q_own))
    loads.append((ids, id_key.at[0, core]))
    loads.append((local.at[0], lq))
    loads.append((local.at[pl.ds(1, 2)], lkv.at[:, pl.ds(tok, tok)]))
    loads = [pltpu.make_async_copy(a, b, load_sem.at[i]) for i, (a, b) in enumerate(loads)]
    for copy in loads:
        copy.start()

    def share(aug, i, h, part, src, sem, device):
        return remote(src, aug.at[part, h, mine, pl.ds(0, DH)], sem, (i, h), seq=device)

    both = ((0, kaug), (1, vaug))
    given = [(i, aug, h, routed.at[1 + i, :, h * DH:(h + 1) * DH]) for h in range(heads) for i, aug in both]
    keys = [share(aug, i, h, 0, src, key_sem, partner) for i, aug, h, src in given]
    keys.append(remote(ids, id_key.at[0, core], kid_sem, (), seq=partner))
    far = [share(aug, i, h, 1, src, far_sem, me + 2) for i, aug, h, src in given if h >= BACK]
    far_id = remote(ids, id_key.at[1, core], fid_sem, (), seq=me + 2)
    near = [share(aug, i, h, 1, aug.at[1, h, mine, pl.ds(0, DH)], near_sem, partner)
            for i, aug, h, src in given if h >= BACK]
    near_id = remote(id_key.at[1, core], id_key.at[1, core], nid_sem, (), seq=partner)

    def halo(r):
        return remote(local.at[pl.ds(1, 2), at(r)], lkv.at[:, at(r)], halo_sem, (r,), seq=me + 1)

    weights = (
        pltpu.make_async_copy(wl_any, wl, w_sem.at[0]),
        pltpu.make_async_copy(wr_any, wr, w_sem.at[1]),
    )

    def q_copy(to, slot, r):
        here = qbuf.at[slot, at(r)]
        if to == 0:
            first = pl.ds(0, BACK * DH)
            here = qbuf.at[slot, at(r), first]
            src = routed.at[0, at(r), first] if slot == 0 else here
        else:
            src = routed.at[0, at(r)]
        return remote(src, here, q_sem, (to, slot, r), seq=2 * to + core)

    def qid_copy(to, slot):
        here = id_query.at[slot]
        return remote(here if to == 0 and slot > 0 else ids, here, qid_sem, (to, slot), seq=2 * to + core)

    def b_copies(r):
        return (remote(bsend.at[r], brecv.at[r], b_sem, (r,), seq=me + 2),
                remote(tsend.at[r], trecv.at[r], t_sem, (r,), seq=me + 2))

    sent = ((1, 1, 2), (1, 2, 3), (2, 2, 3))

    def o_copies(source, slot, r):
        def one(src, dst, sem):
            return pltpu.make_async_remote_copy(
                src_ref=src.at[slot, r], dst_ref=dst.at[source, r],
                send_sem=sem.at[0, slot, r], recv_sem=sem.at[1, source, r],
                device_id={"seq": 2 * (slot + 2) + core}, device_id_type=MESH)

        return one(osend, orecv, o_sem), one(ssend, srecv, s_sem)

    def r_copy(kind, r, half):
        device = across[half] if kind < 2 else across[1 - half]
        return remote(rsend.at[kind, r, half], rrecv.at[kind, r, half], r_sem, (kind, r, half), heads=device)

    pl.semaphore_wait(barrier, greeted)

    @pl.when(z == 0)
    def _():
        far_id.start()
        for copy in far:
            copy.start()

    @pl.when(z == 1)
    def _():
        qid_copy(0, 0).start()

    for to, slot, chip in sent:
        guarded(z == chip, qid_copy(to, slot).start)

    for copy in keys:
        copy.start()

    def ask(r, _):
        for to, slot, chip in sent + ((0, 0, 1),):
            guarded(z == chip, q_copy(to, slot, r).start)

        guarded((me < n - 1) & (me != 1), halo(r).start)
        return 0

    lax.fori_loop(0, rounds, ask, 0)
    for copy in weights:
        copy.start()

    def table(row, on, off):
        c = lax.broadcasted_iota(jnp.int32, (CLUSTERS, tok), 0)
        t = jnp.where(c == row, jnp.float32(on), jnp.float32(off))
        return jnp.transpose(t).astype(jnp.bfloat16)

    def mask_of(slot, id_ref, count=heads):
        for h in range(count):
            qmask[slot, h] = table(id_ref[h:h + 1, :], 0.0, MASKED)

    def key_table(part, c, first=0):
        where = pl.ds(pl.multiple_of(c * tok, tok), tok)
        for h in range(first, heads):
            kaug[part, h, where, DH:] = table(id_key[part, c, h:h + 1, :], 1.0, 0.0)

    for h in range(heads):
        vaug[0, h, :, DH:] = jnp.ones((2 * tok, DH), jnp.bfloat16)

    @pl.when(me == 0)
    def _():
        lkv[:, :tok] = jnp.zeros((2, tok, width), jnp.bfloat16)

    mask_of(0, ids)
    for copy in loads:
        copy.wait()
    key_table(0, core)
    for copy in keys:
        copy.wait_recv()
    key_table(0, 1 - core)

    lane = lax.broadcasted_iota(jnp.int32, (1, DH), 1)

    def softmax(part, h, q, masks, count=None, allowed=None):
        s = dot_nt(jnp.concatenate([q, masks], axis=1), kaug[part, h, :count])
        if allowed is not None:
            own = jnp.where(allowed, s[:rows], MASKED)
            s = own if s.shape[0] == rows else jnp.concatenate([own, s[rows:]], axis=0)
        top = jnp.max(s, axis=-1, keepdims=True)
        p = jnp.exp2((s - top) * SCALE2).astype(jnp.bfloat16)
        o = dot(p, vaug[part, h, :count])
        total = o[:, DH:]
        return o[:, :DH] / total, top * SCALE2 + jnp.log2(total)

    def attend_own(r):
        i = core * tok + start(r) + lax.broadcasted_iota(jnp.int32, (rows, 1), 0)
        for c in range(2):
            @pl.when(core == c)
            def _():
                count = (c + 1) * tok
                allowed = lax.broadcasted_iota(jnp.int32, (1, count), 1) <= i
                stat = jnp.zeros((rows, DH), jnp.float32)
                for h in range(heads):
                    hc = slice(h * DH, (h + 1) * DH)
                    o, level = softmax(0, h, q_own[at(r), hc], qmask[0, h, at(r)], count, allowed)
                    opart[0, at(r), hc] = o
                    stat = jnp.where(lane == h, level, stat)
                spart[0, at(r)] = stat

    def attend(first, r):
        count = 4 - first
        i = core * tok + start(r) + lax.broadcasted_iota(jnp.int32, (rows, 1), 0)
        allowed = lax.broadcasted_iota(jnp.int32, (1, 2 * tok), 1) <= i
        stat = jnp.zeros((rows, DH), jnp.float32)
        stats = jnp.zeros((count * rows, DH), jnp.float32)
        for h in range(heads):
            hc = slice(h * DH, (h + 1) * DH)
            q, masks = q_own[at(r), hc], qmask[0, h, at(r)]
            others = first > 1 or h < BACK
            if others:
                q = jnp.concatenate([q, qbuf[first - 1:, at(r), hc].reshape(count * rows, DH)], axis=0)
                masks = jnp.concatenate([masks, qmask[first:, h, at(r)].reshape(count * rows, DH)], axis=0)
            o, level = softmax(0, h, q, masks, None, allowed)
            if first == 1:
                x[at(r), hc] = o[:rows].astype(jnp.bfloat16)
            else:
                opart[0, at(r), hc] = o[:rows]
                stat = jnp.where(lane == h, level[:rows], stat)
            if others:
                o = o[rows:]
                if first == 1:
                    bsend[r, :, :, hc] = o.astype(jnp.bfloat16).reshape(count, rows, DH)
                elif first == 3:
                    osend[1, r, :, hc] = o.astype(jnp.bfloat16)
                else:
                    opart[1:, at(r), hc] = o.reshape(count, rows, DH)
                stats = jnp.where(lane == h, level[rows:], stats)
            if h == BACK - 1 and first == 1:
                for i in range(count):
                    tsend[r, i] = stat_rows(stats[i * rows:(i + 1) * rows])
                for copy in b_copies(r):
                    copy.start()
        if first > 1:
            spart[0, at(r)] = stat
        if first == 3:
            ssend[1, r] = stat_rows(stats)
            for copy in o_copies(1, 1, r):
                copy.start()
        elif first == 2:
            spart[1:, at(r)] = stats.reshape(count, rows, DH)

    def attend_far(r):
        stat = jnp.zeros((3 * rows, DH), jnp.float32)
        before = spart[:, at(r)].reshape(3 * rows, DH)
        levels_back = jnp.concatenate([stat_columns(trecv[r, i]) for i in range(3)], axis=0)
        for h in range(heads):
            hc = slice(h * DH, (h + 1) * DH)
            if h < BACK:
                o = brecv[r, :, :, hc].reshape(3 * rows, DH).astype(jnp.float32)
                level = levels_back[:, h:h + 1]
            else:
                q = jnp.concatenate([q_own[at(r), hc], qbuf[1:, at(r), hc].reshape(2 * rows, DH)], axis=0)
                masks = jnp.concatenate([qmask[0, h, at(r)], qmask[2:, h, at(r)].reshape(2 * rows, DH)], axis=0)
                o, level = softmax(1, h, q, masks)
            level_near = before[:, h:h + 1]
            high = jnp.maximum(level, level_near)
            w = jnp.exp2(level - high)
            w_near = jnp.exp2(level_near - high)
            total = w + w_near
            o = ((w * o + w_near * opart[:, at(r), hc].reshape(3 * rows, DH)) / total).astype(jnp.bfloat16)
            x[at(r), hc] = o[:rows]
            for slot in range(2):
                osend[slot, r, :, hc] = o[(slot + 1) * rows:(slot + 2) * rows]
            stat = jnp.where(lane == h, high + jnp.log2(total), stat)
        for slot in (1, 0):
            ssend[slot, r] = stat_rows(stat[(slot + 1) * rows:(slot + 2) * rows])
            for copy in o_copies(0, slot, r):
                copy.start()

    def stat_columns(packed):
        return jnp.transpose(jnp.concatenate([packed, jnp.zeros((DH - 8, DH), jnp.float32)], axis=0))[:rows]

    def stat_rows(stat):
        return jnp.transpose(jnp.concatenate([stat] * (DH // rows), axis=0))[:8]

    def window(r):
        i = lax.broadcasted_iota(jnp.int32, (rows, rows + WINDOW), 0)
        c = lax.broadcasted_iota(jnp.int32, (rows, rows + WINDOW), 1)
        lowest = jnp.where(me == 0, WINDOW - start(r), 0)
        allowed = (c > i) & (c <= i + WINDOW) & (c >= lowest)
        span = pl.ds(pl.multiple_of(start(r), rows), rows + WINDOW)
        guarded(me > 0, halo(r).wait_recv)

        def head(h, _):
            hc = pl.ds(pl.multiple_of(h * DH, DH), DH)
            s = jnp.where(allowed, dot_nt(lq[at(r), hc], lkv[0, span, hc]), MASKED)
            top = jnp.max(s, axis=-1, keepdims=True)
            p = jnp.exp2((s - top) * SCALE2)
            total = jnp.sum(p, axis=-1, keepdims=True)
            o = dot(p.astype(jnp.bfloat16), lkv[1, span, hc]) / total
            lout[at(r), hc] = o.astype(jnp.bfloat16)
            return 0

        lax.fori_loop(0, heads, head, 0, unroll=True)

    def merge(sources, r):
        levels = [spart[0, at(r)]]
        for source in sources:
            for copy in o_copies(source, 0, r):
                copy.wait_recv()
            levels.append(stat_columns(srecv[source, r]))
        high = functools.reduce(jnp.maximum, levels)
        ws = [jnp.exp2(level - high) for level in levels]
        total = sum(ws[1:], ws[0])
        ws = [w / total for w in ws]
        for h in range(heads):
            hc = slice(h * DH, (h + 1) * DH)
            o = ws[0][:, h:h + 1] * opart[0, at(r), hc]
            for source, w in zip(sources, ws[1:]):
                o = o + w[:, h:h + 1] * orecv[source, r, :, hc].astype(jnp.float32)
            x[at(r), hc] = o.astype(jnp.bfloat16)

    def product(owner, half, r):
        c = pl.ds(pl.multiple_of(owner * cols + half * half_cols, half_cols), half_cols)
        return dot(lout[at(r)], wl[:, c]) + dot(x[at(r)], wr[:, c])

    def hand(kind, r, half, value):
        rsend[kind, r, half] = value.astype(jnp.bfloat16)
        r_copy(kind, r, half).start()

    def reduce1(r):
        for half in range(2):
            hand(0, r, half, product(corner, half, r))
        for half in range(2):
            hand(1, r, half, product(across[half], half, r))

    def reduce2(r):
        for half in range(2):
            value = product(across[1 - half], half, r)
            r_copy(0, r, half).wait_recv()
            hand(2, r, half, value + rrecv[0, r, half].astype(jnp.float32))

    def reduce3(r):
        for half in range(2):
            value = product(place, half, r)
            for kind in (1, 2):
                r_copy(kind, r, half).wait_recv()
                value = value + rrecv[kind, r, half].astype(jnp.float32)
            out_ref[at(r), half * half_cols:(half + 1) * half_cols] = value.astype(jnp.bfloat16)

    def reduce_late():
        def step(t, _):
            guarded(t < rounds, reduce2, t)
            guarded(t >= 1, reduce3, t - 1)
            return 0

        lax.fori_loop(0, rounds + 1, step, 0)

    def both_weights():
        for copy in weights:
            copy.wait()

    @pl.when(z == 0)
    def _():
        def step(t, _):
            for slot in range(3):
                q_copy(0, slot, t).wait_recv()
            attend(1, t)
            guarded(me == 1, halo(t).start)
            window(t)
            guarded(t == 0, both_weights)
            reduce1(t)
            return 0

        for slot in range(3):
            qid_copy(0, slot).wait_recv()
            mask_of(1 + slot, id_query.at[slot], BACK)
        lax.fori_loop(0, rounds, step, 0)
        reduce_late()
        far_id.wait_send()
        for copy in far:
            copy.wait_send()

    @pl.when(z == 1)
    def _():
        for slot in (1, 2):
            qid_copy(1, slot).wait_recv()
            qid_copy(0, slot).start()
            mask_of(1 + slot, id_query.at[slot])
        vaug[1, BACK:, :, DH:] = vaug[0, BACK:, :, DH:]

        def first(t, _):
            for slot in (1, 2):
                q_copy(1, slot, t).wait_recv()
                q_copy(0, slot, t).start()
            attend(2, t)
            return 0

        lax.fori_loop(0, rounds, first, 0)
        far_id.wait_recv()
        near_id.start()
        key_table(1, core, BACK)
        for here, there in zip(far, near):
            here.wait_recv()
            there.start()
        near_id.wait_recv()
        key_table(1, 1 - core, BACK)
        for copy in near:
            copy.wait_recv()
        both_weights()

        def second(t, _):
            for copy in b_copies(t):
                copy.wait_recv()
            attend_far(t)
            window(t)
            reduce1(t)
            return 0

        lax.fori_loop(0, rounds, second, 0)
        reduce_late()
        near_id.wait_send()
        for copy in near:
            copy.wait_send()

    @pl.when(z >= 2)
    def _():
        @pl.when(z == 2)
        def _():
            qid_copy(2, 2).wait_recv()
            mask_of(3, id_query.at[2])

        def first(t, _):
            @pl.when(z == 2)
            def _():
                q_copy(2, 2, t).wait_recv()
                attend(3, t)

            guarded(z == 3, attend_own, t)
            return 0

        lax.fori_loop(0, rounds, first, 0)

        def second(t, _):
            window(t)
            return 0

        lax.fori_loop(0, rounds, second, 0)
        both_weights()

        def third(t, _):
            guarded((t >= 1) & (t <= rounds), lambda: reduce2(t - 1))

            @pl.when(t < rounds)
            def _():
                guarded(z == 2, merge, (0,), t)
                guarded(z == 3, merge, (0, 1), t)
                reduce1(t)

            guarded(t >= 2, lambda: reduce3(t - 2))
            return 0

        lax.fori_loop(0, rounds + 2, third, 0)

    for copy in keys:
        copy.wait_send()

    sent = sent + ((0, 0, 1), (0, 1, 1), (0, 2, 1))
    for to, slot, chip in sent:
        guarded(z == chip, qid_copy(to, slot).wait_send)

    def settle(r, _):
        for to, slot, chip in sent:
            guarded(z == chip, q_copy(to, slot, r).wait_send)
        guarded(me < n - 1, halo(r).wait_send)

        @pl.when(z == 0)
        def _():
            for copy in b_copies(r):
                copy.wait_send()

        for slot in range(2):
            @pl.when((z == 1) | ((z == 2) & (slot == 1)))
            def _():
                for copy in o_copies(0, slot, r):
                    copy.wait_send()

        return 0

    lax.fori_loop(0, rounds, settle, 0)

    def settle_sums(r, _):
        for kind in range(3):
            for half in range(2):
                r_copy(kind, r, half).wait_send()
        return 0

    lax.fori_loop(0, rounds, settle_sums, 0)


def chain_body(local_qkv, routed_qkv, clusters, wo_local, wo_routed):
    tok, width = routed_qkv.shape[1:]
    heads = clusters.shape[0]
    n = lax.axis_size("seq")
    rows = tok // ROUNDS
    cols = wo_local.shape[1] // lax.axis_size("heads")
    DMA = pltpu.SemaphoreType.DMA
    any_spec = pl.BlockSpec(memory_space=pl.ANY)

    def bf16(*shape):
        return pltpu.VMEM(shape, jnp.bfloat16)

    def f32(*shape):
        return pltpu.VMEM(shape, jnp.float32)

    slots = (3, ROUNDS, 2, rows, cols // 2)
    return pl.pallas_call(
        functools.partial(chain_kernel, n),
        out_shape=jax.ShapeDtypeStruct((tok, cols), jnp.bfloat16),
        in_specs=[any_spec, vmem(), any_spec, any_spec, any_spec],
        out_specs=vmem(),
        scratch_shapes=[
            bf16(2, heads, 2 * tok, 2 * DH), bf16(2, heads, 2 * tok, 2 * DH),
            bf16(tok, width), bf16(3, tok, width), bf16(4, heads, tok, CLUSTERS),
            pltpu.VMEM((2, 2, heads, tok), jnp.int32), pltpu.VMEM((3, heads, tok), jnp.int32),
            f32(3, tok, width), f32(3, tok, DH),
            bf16(2, ROUNDS, rows, width), bf16(2, ROUNDS, rows, width),
            f32(2, ROUNDS, 8, DH), f32(2, ROUNDS, 8, DH),
            bf16(ROUNDS, 3, rows, BACK * DH), bf16(ROUNDS, 3, rows, BACK * DH),
            f32(ROUNDS, 3, 8, DH), f32(ROUNDS, 3, 8, DH),
            bf16(tok, width), bf16(2, 2 * tok, width), bf16(tok, width), bf16(tok, width),
            bf16(*wo_local.shape), bf16(*wo_routed.shape), bf16(*slots), bf16(*slots),
            DMA((2 * heads + 4,)), DMA((2, 2, heads)), DMA((2,)), DMA((2, 2, heads)), DMA((2,)),
            DMA((2, 2, heads)), DMA((2,)), DMA((2, 3, 3, ROUNDS)), DMA((2, 3, 3)),
            DMA((2, 2, ROUNDS)), DMA((2, 2, ROUNDS)), DMA((2, ROUNDS)), DMA((2, ROUNDS)),
            DMA((2, ROUNDS)), DMA((2,)), DMA((2,) + slots[:3]),
        ],
        cost_estimate=pl.CostEstimate(
            flops=8 << 30, bytes_accessed=20 << 20, transcendentals=8 << 20),
        compiler_params=pltpu.CompilerParams(
            vmem_limit_bytes=VMEM_LIMIT, collective_id=1, has_side_effects=True),
    )(routed_qkv, clusters, local_qkv, wo_local, wo_routed)


def solution(mesh):
    return jax.shard_map(
        chain_body if mesh.shape["seq"] == 8 else body,
        mesh=mesh,
        in_specs=(
            P(None, "seq", "heads"),
            P(None, "seq", "heads"),
            P("heads", "seq"),
            P("heads", None),
            P("heads", None),
        ),
        out_specs=P("seq", "heads"),
        check_vma=False,
    )
```
